32 devices in a mesh: gx: 8 (over y, x, core), gy: 4 (over z).
Axes of the slice: x: 2, y: 2, z: 4, core: 2. Of those that a mesh axis runs over, the one named last changes fastest.
Arguments:
- composition: float32 [53, 262144], P(None, ('gx', 'gy')), may hold values from -6 to 6
- particle_mass: float32 [262144], P(('gx', 'gy')), may hold values from 0.3 to 3
- particle_cell: int32 [2, 262144], P(None, ('gx', 'gy')), may hold values from 0 to 511, as said below
- particle_level: int32 [262144], P(('gx', 'gy')), may hold values from 0 to 2, as said below
- les_mean: float32 [53, 32, 512], P(None, 'gx', 'gy'), may hold values from -6 to 6
- mix_rate: float32 [32, 512], P('gx', 'gy'), may hold values from 0.1 to 3
- rate_matrix: float32 [3, 53, 53], replicated, may hold values from -0.875 to 0.875
- implicit_map: float32 [3, 53, 53], replicated, may hold values from -0.875 to 0.875
Outputs:
- updated: float32 [53, 262144], P(None, ('gx', 'gy'))
- cell_means: float32 [53, 32, 512], P(None, 'gx', 'gy')
The draws below stay inside these ranges and needn't reach their ends.
Inputs may be any that keep to these rules, and one draw needn't show every extreme that they name: `particle_cell`: row 0 is below 32 and row 1 below 512. With the cells split into blocks of 4 x 128 cells in device order (streamwise block index major), every particle's cell lies within 2 cells, in each grid direction, of the block of the device that holds the particle; the distance 2 is reached on every side that has a neighbouring block. `particle_level`: the share of full-mechanism particles differs from device to device, from none to all.
All inputs are finite; a program needn't handle non-finite values.
Results may differ from the reference program's by a relative error of at most 0.0001.
Values sent between devices are 32-bit elements; how exact they have to be, the bound alone decides.
A program may use at most 64 MiB of HBM per device.

```python
import math
import jax
import jax.numpy as jnp
from jax import lax

NSP = 53
NS_LOW = 21
NS_MID = 24
CX = 4
CY = 128
R = 2
P_DEV = 8192
P_TOTAL = 262144
NX = 32
NY = 512


def draw_particle_cell(key, part):
    grid_rows = NY // CY
    device_id = jnp.arange(P_TOTAL, dtype=jnp.int32) // P_DEV
    column_index = device_id // grid_rows
    row_index = device_id % grid_rows
    key_flagx, key_flagy, key_cellx, key_celly = jax.random.split(key, 4)
    spread_x = jax.random.randint(key_flagx, (P_TOTAL,), 0, 4) == 0
    spread_y = jax.random.randint(key_flagy, (P_TOTAL,), 0, 4) == 0
    lower_x = jnp.where(spread_x, jnp.maximum(column_index * CX - R, 0), column_index * CX)
    upper_x = jnp.where(spread_x, jnp.minimum(column_index * CX + CX + R, NX), column_index * CX + CX)
    lower_y = jnp.where(spread_y, jnp.maximum(row_index * CY - R, 0), row_index * CY)
    upper_y = jnp.where(spread_y, jnp.minimum(row_index * CY + CY + R, NY), row_index * CY + CY)
    cell_x = jax.random.randint(key_cellx, (P_TOTAL,), lower_x, upper_x)
    cell_y = jax.random.randint(key_celly, (P_TOTAL,), lower_y, upper_y)
    return jnp.stack([cell_x, cell_y], 0).astype(jnp.int32)


def draw_particle_level(key, part):
    key_device, key_pick, key_lower = jax.random.split(key, 3)
    device_total = NX // CX * (NY // CY)
    flame_share = jax.random.randint(key_device, (device_total,), 0, 9)
    device_id = jnp.arange(P_TOTAL, dtype=jnp.int32) // P_DEV
    share_each = jnp.take(flame_share, device_id)
    picked = jax.random.randint(key_pick, (P_TOTAL,), 0, 8)
    lower_level = jax.random.randint(key_lower, (P_TOTAL,), 0, 2)
    return jnp.where(picked < share_each, 2, lower_level).astype(jnp.int32)


def level_of(own_key, extent, cuts, smallest, high):
    level, own = 1.0, jax.random.fold_in(own_key, 6)
    for position, shards_of in cuts:
        draws = jnp.exp(jax.random.uniform(jax.random.fold_in(own, position), (shards_of,), jnp.float32, smallest / len(cuts), high / len(cuts)))
        level = level * jnp.repeat(draws, extent[position] // shards_of).reshape([-1 if axis == position else 1 for axis in range(len(extent))])
    return level


def normal_values(rng, extent, scale, bound, cuts=(), kind=jnp.bfloat16):
    result = scale * jax.random.normal(rng, extent, jnp.float32)
    if cuts:
        result = result * level_of(rng, extent, cuts, -0.22, 0.18)
    return jnp.clip(result, -bound, bound).astype(kind)


def setup_inputs(seed: int = 0) -> dict:
    key_of = jax.random.split(jax.random.key(seed), 9)
    composition = normal_values(key_of[0], (NSP, P_TOTAL), 1.0, 6.0, ((1, 32),), jnp.float32)
    particle_mass = jnp.clip(jnp.exp(math.log(3.0) - 2.3025851 * jax.random.uniform(key_of[1], (P_TOTAL,), jnp.float32) ** level_of(key_of[1], (P_TOTAL,), ((0, 32),), -0.2, 0.2)), 0.3, 3.0)
    particle_cell = draw_particle_cell(jax.random.fold_in(key_of[8], 71), 0)
    particle_level = draw_particle_level(jax.random.fold_in(key_of[8], 71), 0)
    les_mean = normal_values(key_of[4], (NSP, NX, NY), 1.0, 6.0, ((1, 8), (2, 4)), jnp.float32)
    mix_rate = jnp.clip(jnp.exp(math.log(3.0) - 3.4011974 * jax.random.uniform(key_of[5], (NX, NY), jnp.float32) ** level_of(key_of[5], (NX, NY), ((0, 8), (1, 4)), -0.2, 0.2)), 0.1, 3.0)
    rate_matrix = normal_values(key_of[6], (3, NSP, NSP), NSP ** -0.5, 0.875, (), jnp.float32)
    implicit_map = normal_values(key_of[7], (3, NSP, NSP), NSP ** -0.5, 0.875, (), jnp.float32)
    return dict(composition=composition, particle_mass=particle_mass, particle_cell=particle_cell, particle_level=particle_level, les_mean=les_mean, mix_rate=mix_rate, rate_matrix=rate_matrix, implicit_map=implicit_map)


prior_weight = 16.0
chem_step = 0.5


def react(mixed_comp, rate_matrix, implicit_map, particle_level):
    updated = mixed_comp
    for tier_index, active in enumerate((NS_LOW, NS_MID, NSP)):
        block_comp = mixed_comp[:active]
        source = jnp.tanh(jnp.dot(rate_matrix[tier_index, :active, :active], block_comp, precision=lax.Precision.HIGHEST, preferred_element_type=jnp.float32))
        change = jnp.dot(implicit_map[tier_index, :active, :active], source, precision=lax.Precision.HIGHEST, preferred_element_type=jnp.float32)
        change = jnp.concatenate([change, jnp.zeros((NSP - active, change.shape[1]), jnp.float32)], 0)
        updated = updated + jnp.where(particle_level[None, :] == tier_index, chem_step * change, 0.0)
    return updated


def reference(composition, particle_mass, particle_cell, particle_level, les_mean, mix_rate, rate_matrix, implicit_map):
    cell_count = NX * NY
    flat_cell = (particle_cell[0] * NY + particle_cell[1]).astype(jnp.int32)
    weighted = composition * particle_mass[None, :]
    weighted_sums = jax.ops.segment_sum(weighted.T, flat_cell, num_segments=cell_count).T.reshape(NSP, NX, NY)
    mass_sums = jax.ops.segment_sum(particle_mass, flat_cell, num_segments=cell_count).reshape(1, NX, NY)
    cell_means = (weighted_sums + prior_weight * les_mean) / (mass_sums + prior_weight)
    particle_means = jnp.take(cell_means.reshape(NSP, cell_count), flat_cell, axis=1)
    particle_rate = jnp.take(mix_rate.reshape(cell_count), flat_cell, axis=0)
    factor = 1.0 - jnp.exp(-particle_rate)
    mixed_comp = composition - factor[None, :] * (composition - particle_means)
    updated = react(mixed_comp, rate_matrix, implicit_map, particle_level)
    return updated, cell_means
```

```python
import functools

import jax
import jax.numpy as jnp
from jax import lax
from jax.experimental import pallas as pl
from jax.experimental.pallas import tpu as pltpu
from jax.sharding import PartitionSpec as P

NS_LOW = 21
NS_MID = 24
R = 2
W = 2 * R
HALF = 64
ROWS = 56
LANES = 128

prior_weight = 16.0
chem_step = 0.5
BF = jnp.bfloat16
F32 = jnp.float32
MESH = pl.DeviceIdType.MESH


def halves(value):
    high = value.astype(BF)
    return high, (value - high.astype(F32)).astype(BF)


def roll(value, shift):
    return pltpu.roll(value, shift % value.shape[1], 1)


def fill_one_hot(one_hot, cell, block_x, block_y):
    span_x = block_x + 2 * R
    count = cell.shape[1]
    local_x = cell[0:1] - (lax.axis_index("gx") * block_x - R)
    local_y = cell[1:2] - (lax.axis_index("gy") * block_y - R)
    low_rim = local_y < W
    high_rim = local_y >= block_y
    rim = jnp.where(low_rim, local_y, local_y - block_y + span_x * W) + local_x * W
    inner = jnp.where(low_rim | high_rim, -1, local_y - R)
    rim = jnp.where(low_rim | high_rim, rim, -1)
    sub = lax.broadcasted_iota(jnp.int32, (block_y, count), 0)
    hot_y = jnp.where(sub == inner, 1.0, 0.0).astype(BF)
    for x in range(span_x):
        hot_x = jnp.broadcast_to(jnp.where(local_x == x, 1.0, 0.0), (block_y, count))
        one_hot[x * block_y : (x + 1) * block_y, :] = hot_y * hot_x.astype(BF)
    sub = lax.broadcasted_iota(jnp.int32, (LANES, count), 0)
    one_hot[span_x * block_y : span_x * block_y + LANES, :] = jnp.where(
        sub == rim, 1.0, 0.0
    ).astype(BF)


def scatter_kernel(block_x, block_y, comp, mass, cell, sums, one_hot, weighted):
    species = comp.shape[0]

    @pl.when(pl.program_id(0) == 0)
    def _():
        sums[...] = jnp.zeros_like(sums)
        weighted[...] = jnp.zeros_like(weighted)

    weighted[0:species, :] = comp[...] * mass[...]
    weighted[species : species + 1, :] = mass[...]
    high, low = halves(weighted[...])
    fill_one_hot(one_hot, cell[...], block_x, block_y)
    sums[...] += lax.dot_general(
        jnp.concatenate([high, low], 0),
        one_hot[...],
        (((1,), (1,)), ((), ())),
        preferred_element_type=F32,
    )


def exchange_kernel(
    counts, species, block_x, block_y, sums, les, rate, table, means,
    send, own, from_x, from_y, from_xy, wide, send_main, recv_main, send_rim, recv_rim,
):
    span_x = block_x + 2 * R
    gx, gy = lax.axis_index("gx"), lax.axis_index("gy")
    has = {
        -1: (gx > 0, gy > 0),
        1: (gx < counts[0] - 1, gy < counts[1] - 1),
        0: (True, True),
    }
    others = [(dx, dy) for dx in (-1, 0, 1) for dy in (-1, 0, 1) if (dx, dy) != (0, 0)]

    def present(dx, dy):
        return jnp.logical_and(has[dx][0], has[dy][1])

    barrier = pltpu.get_barrier_semaphore()
    for dx, dy in others:
        @pl.when(present(dx, dy))
        def _():
            pl.semaphore_signal(
                barrier, inc=1, device_id=(gx + dx, gy + dy), device_id_type=MESH
            )

    lane = lax.broadcasted_iota(jnp.int32, (ROWS, LANES), 1)
    lane_y = lax.broadcasted_iota(jnp.int32, (ROWS, block_y), 1)
    inside = (lane_y >= R) & (lane_y < block_y - R)
    for x in range(span_x + 1):
        at = x * block_y
        width = block_y if x < span_x else LANES
        send[x] = sums[0:ROWS, at : at + width] + sums[HALF : HALF + ROWS, at : at + width]
    own[...] = jnp.zeros_like(own)
    rim_prior = jnp.zeros((ROWS, LANES), F32)
    for x in range(block_x):
        t = x + R
        own[0:species, :] = prior_weight * les[:, x, :]
        own[species : species + 1, :] = jnp.full((1, block_y), prior_weight, F32)
        own[species + 1 : species + 2, :] = 1.0 - jnp.exp(-rate[x : x + 1, :])
        prior = own[...]
        send[t] += jnp.where(inside, prior, 0.0)
        low_at, high_at = t * W + R, (span_x + t) * W
        low = roll(prior, low_at)
        high = roll(prior, high_at + R)
        rim_prior += jnp.where((lane >= low_at) & (lane < low_at + R), low, 0.0)
        rim_prior += jnp.where((lane >= high_at) & (lane < high_at + R), high, 0.0)
    send[span_x] += rim_prior

    number = (1 + (gx > 0).astype(jnp.int32) + (gx < counts[0] - 1).astype(jnp.int32)) * (
        1 + (gy > 0).astype(jnp.int32) + (gy < counts[1] - 1).astype(jnp.int32)
    ) - 1
    pl.semaphore_wait(barrier, number)

    def landing(dx, dy):
        if dy == 0:
            return from_x.at[(dx + 1) // 2, W]
        if dx == 0:
            return from_y.at[(dy + 1) // 2]
        return from_xy.at[(dx + 1) // 2, (dy + 1) // 2]

    def main_copy(dx):
        first = 0 if dx < 0 else block_x
        return pltpu.make_async_remote_copy(
            src_ref=send.at[pl.ds(first, W)],
            dst_ref=from_x.at[(1 - dx) // 2, pl.ds(0, W)],
            send_sem=send_main.at[(dx + 1) // 2],
            recv_sem=recv_main.at[(1 - dx) // 2],
            device_id=(gx + dx, gy),
            device_id_type=MESH,
        )

    def rim_copy(k, dx, dy):
        return pltpu.make_async_remote_copy(
            src_ref=send.at[span_x],
            dst_ref=landing(-dx, -dy),
            send_sem=send_rim.at[k],
            recv_sem=recv_rim.at[len(others) - 1 - k],
            device_id=(gx + dx, gy + dy),
            device_id_type=MESH,
        )

    for k, (dx, dy) in enumerate(others):
        @pl.when(present(dx, dy))
        def _():
            rim_copy(k, dx, dy).start()
    for dx in (-1, 1):
        @pl.when(has[dx][0])
        def _():
            main_copy(dx).start()

        @pl.when(jnp.logical_not(has[dx][0]))
        def _():
            from_x[(dx + 1) // 2] = jnp.zeros((W + 1, ROWS, LANES), F32)
    for dx, dy in others:
        if dy != 0:
            @pl.when(jnp.logical_not(present(dx, dy)))
            def _():
                landing(dx, dy)[...] = jnp.zeros((ROWS, LANES), F32)

    for k, (dx, dy) in enumerate(others):
        @pl.when(present(dx, dy))
        def _():
            pltpu.make_async_remote_copy(
                src_ref=send.at[span_x],
                dst_ref=landing(dx, dy),
                send_sem=send_rim.at[k],
                recv_sem=recv_rim.at[k],
                device_id=(gx + dx, gy + dy),
                device_id_type=MESH,
            ).wait_recv()
    for dx in (-1, 1):
        @pl.when(has[dx][0])
        def _():
            pltpu.make_async_remote_copy(
                src_ref=send.at[pl.ds(0, W)],
                dst_ref=from_x.at[(dx + 1) // 2, pl.ds(0, W)],
                send_sem=send_main.at[(dx + 1) // 2],
                recv_sem=recv_main.at[(dx + 1) // 2],
                device_id=(gx + dx, gy),
                device_id_type=MESH,
            ).wait_recv()

    row = lax.broadcasted_iota(jnp.int32, (ROWS, LANES), 0)
    wide[...] = jnp.zeros_like(wide)

    def finish(total, x):
        mass = total[species : species + 1, :]
        weight = jnp.broadcast_to(jnp.where(mass > 0.0, mass, 1.0), total.shape)
        value = total / jnp.where(row < species, weight, 1.0)
        wide[0:ROWS, :] = value
        high, low = halves(wide[...])
        table[0:HALF, x * block_y : x * block_y + LANES] = high
        table[HALF:, x * block_y : x * block_y + LANES] = low
        return value

    side_size = span_x * W
    low_side = lane < side_size
    place_x = jnp.where(low_side, lane, lane - side_size)
    used = lane < 2 * side_size
    behind = used & (place_x < 2 * R * W)
    ahead = used & (place_x >= block_x * W)
    step = block_x * W
    total = send[span_x]
    for dx in (-1, 0, 1):
        for dy in (-1, 0, 1):
            if (dx, dy) == (0, 0):
                continue
            mask = used if dx == 0 else behind if dx < 0 else ahead
            if dy != 0:
                mask = mask & (low_side if dy < 0 else jnp.logical_not(low_side))
            shift = dx * step + dy * side_size
            total = total + jnp.where(mask, roll(landing(dx, dy)[...], shift), 0.0)
    rim_value = finish(total, span_x)
    for t in range(span_x):
        total = send[t]
        if t < W:
            total = total + from_x[0, t]
        if t >= block_x:
            total = total + from_x[1, t - block_x]
        value = finish(total, t)
        if R <= t < R + block_x:
            low_at, high_at = t * W + R, (span_x + t) * W
            value = jnp.where(lane_y < R, roll(rim_value, -low_at), value)
            value = jnp.where(
                lane_y >= block_y - R, roll(rim_value, block_y - R - high_at), value
            )
            means[:, t - R, :] = value[0:species]

    for k, (dx, dy) in enumerate(others):
        @pl.when(present(dx, dy))
        def _():
            rim_copy(k, dx, dy).wait_send()
    for dx in (-1, 1):
        @pl.when(has[dx][0])
        def _():
            main_copy(dx).wait_send()


def stack_levels(target, plain, matrices):
    species = matrices.shape[1]
    plain[...] = jnp.zeros_like(plain)
    plain[0:species, 0:species] = matrices[2]
    plain[HALF : HALF + NS_MID, 0:NS_MID] = matrices[1, 0:NS_MID, 0:NS_MID]
    base = HALF + NS_MID
    plain[base : base + NS_LOW, 0:NS_LOW] = matrices[0, 0:NS_LOW, 0:NS_LOW]
    high, low = halves(plain[...])
    target[:, 0:HALF] = high
    target[:, HALF : 2 * HALF] = high
    target[:, 2 * HALF :] = low


def react_kernel(
    block_x, block_y, comp, cell, level, table, rate, implicit, out,
    one_hot, mixed, plain, left_rate, left_implicit,
):
    species = comp.shape[0]

    @pl.when(pl.program_id(0) == 0)
    def _():
        mixed[...] = jnp.zeros_like(mixed)
        stack_levels(left_rate, plain, rate)
        stack_levels(left_implicit, plain, implicit)

    fill_one_hot(one_hot, cell[...], block_x, block_y)
    both = jnp.dot(table[...], one_hot[...], preferred_element_type=F32)
    taken = both[0:HALF] + both[HALF:]
    factor = taken[species + 1 : species + 2]
    comp_value = comp[...]
    mixed[0:species, :] = comp_value - factor * (comp_value - taken[0:species])
    levels = level[...]
    full, middle = levels == 2, levels == 1
    high, low = halves(mixed[...])
    right = jnp.concatenate([high, low, high], 0)
    drive = jnp.dot(left_rate[...], right, preferred_element_type=F32)
    base = HALF + NS_MID
    top = jnp.where(
        full, drive[0:NS_MID],
        jnp.where(middle, drive[HALF:base], drive[base : base + NS_MID]),
    )
    source = jnp.tanh(jnp.concatenate([top, drive[NS_MID:HALF]], 0))
    high, low = halves(source)
    right = jnp.concatenate([high, low, high], 0)
    change = jnp.dot(left_implicit[...], right, preferred_element_type=F32)
    top = jnp.where(
        full, change[0:NS_MID],
        jnp.where(middle, change[HALF:base], change[base : base + NS_MID]),
    )
    rest = jnp.where(full, change[NS_MID:species], 0.0)
    out[0:NS_MID, :] = mixed[0:NS_MID, :] + chem_step * top
    out[NS_MID:, :] = mixed[NS_MID:species, :] + chem_step * rest


def per_device(
    counts, composition, particle_mass, particle_cell, particle_level,
    les_mean, mix_rate, rate_matrix, implicit_map,
):
    species, particles = composition.shape
    block_x, block_y = les_mean.shape[1], les_mean.shape[2]
    span_x = block_x + 2 * R
    columns = span_x * block_y + LANES
    chunk = 1024
    steps = particles // chunk
    whole = pl.BlockSpec(memory_space=pltpu.VMEM)

    def by_chunk(rows):
        return pl.BlockSpec((rows, chunk), lambda i: (0, i))

    params = pltpu.CompilerParams(vmem_limit_bytes=48 << 20)
    sums = pl.pallas_call(
        functools.partial(scatter_kernel, block_x, block_y),
        grid=(steps,),
        out_shape=jax.ShapeDtypeStruct((2 * HALF, columns), F32),
        in_specs=[by_chunk(species), by_chunk(1), by_chunk(2)],
        out_specs=pl.BlockSpec((2 * HALF, columns), lambda i: (0, 0)),
        scratch_shapes=[pltpu.VMEM((columns, chunk), BF), pltpu.VMEM((HALF, chunk), F32)],
        compiler_params=params,
    )(composition, particle_mass[None], particle_cell)
    dma = pltpu.SemaphoreType.DMA
    table, means = pl.pallas_call(
        functools.partial(exchange_kernel, counts, species, block_x, block_y),
        out_shape=(
            jax.ShapeDtypeStruct((2 * HALF, columns), BF),
            jax.ShapeDtypeStruct(les_mean.shape, F32),
        ),
        in_specs=[whole] * 3,
        out_specs=(whole, whole),
        scratch_shapes=[
            pltpu.VMEM((span_x + 1, ROWS, LANES), F32),
            pltpu.VMEM((ROWS, block_y), F32),
            pltpu.VMEM((2, W + 1, ROWS, LANES), F32),
            pltpu.VMEM((2, ROWS, LANES), F32),
            pltpu.VMEM((2, 2, ROWS, LANES), F32),
            pltpu.VMEM((HALF, LANES), F32),
            dma((2,)), dma((2,)), dma((8,)), dma((8,)),
        ],
        compiler_params=pltpu.CompilerParams(collective_id=0, has_side_effects=True),
    )(sums, les_mean, mix_rate)
    stacked = HALF + 2 * NS_MID
    updated = pl.pallas_call(
        functools.partial(react_kernel, block_x, block_y),
        grid=(steps,),
        out_shape=jax.ShapeDtypeStruct(composition.shape, F32),
        in_specs=[by_chunk(species), by_chunk(2), by_chunk(1), whole, whole, whole],
        out_specs=by_chunk(species),
        scratch_shapes=[
            pltpu.VMEM((columns, chunk), BF),
            pltpu.VMEM((HALF, chunk), F32),
            pltpu.VMEM((stacked, HALF), F32),
            pltpu.VMEM((stacked, 3 * HALF), BF),
            pltpu.VMEM((stacked, 3 * HALF), BF),
        ],
        compiler_params=params,
    )(composition, particle_cell, particle_level[None], table, rate_matrix, implicit_map)
    return updated, means


def solution(mesh):
    placed = (
        P(None, ("gx", "gy")),
        P(("gx", "gy")),
        P(None, ("gx", "gy")),
        P(("gx", "gy")),
        P(None, "gx", "gy"),
        P("gx", "gy"),
        P(),
        P(),
    )
    return jax.shard_map(
        functools.partial(per_device, (mesh.shape["gx"], mesh.shape["gy"])),
        mesh=mesh,
        in_specs=placed,
        out_specs=(P(None, ("gx", "gy")), P(None, "gx", "gy")),
        check_vma=False,
    )
```

```python
import functools

import jax
import jax.numpy as jnp
from jax import lax
from jax.experimental import pallas as pl
from jax.experimental.pallas import tpu as pltpu
from jax.sharding import PartitionSpec as P

NS_LOW = 21
NS_MID = 24
R = 2
W = 2 * R
HALF = 64
ROWS = 56
LANES = 128

prior_weight = 16.0
chem_step = 0.5
BF = jnp.bfloat16
F32 = jnp.float32
MESH = pl.DeviceIdType.MESH


def halves(value):
    high = value.astype(BF)
    return high, (value - high.astype(F32)).astype(BF)


def roll(value, shift):
    return pltpu.roll(value, shift % value.shape[1], 1)


def positions(cell, block_x, block_y):
    local_x = cell[0:1] - (lax.axis_index("gx") * block_x - R)
    local_y = cell[1:2] - (lax.axis_index("gy") * block_y - R)
    low_rim = local_y < W
    on_rim = low_rim | (local_y >= block_y)
    rim = jnp.where(low_rim, local_y, local_y - block_y + (block_x + 2 * R) * W) + local_x * W
    return local_x, jnp.where(on_rim, -1, local_y - R), jnp.where(on_rim, rim, -1)


def one_hot(place, rows, period):
    sub = lax.broadcasted_iota(jnp.int32, (rows, place.shape[1]), 0)
    if period < rows:
        sub = sub % period
    return jnp.where(sub == place, 1.0, 0.0).astype(BF)


def sums_kernel(
    counts, steps, chunk, block_x, block_y, comp, mass, cell, les, rate, table, means,
    hot, hot_rim, weighted, split, acc, acc_rim,
    send, prior, from_x, from_y, from_xy, send_main, recv_main, send_rim, recv_rim,
):
    species = comp.shape[0]
    span_x = block_x + 2 * R
    side_size = span_x * W
    gx, gy = lax.axis_index("gx"), lax.axis_index("gy")
    index = pl.program_id(0)
    has = {
        -1: (gx > 0, gy > 0),
        1: (gx < counts[0] - 1, gy < counts[1] - 1),
        0: (True, True),
    }
    others = [(dx, dy) for dx in (-1, 0, 1) for dy in (-1, 0, 1) if (dx, dy) != (0, 0)]
    lane = lax.broadcasted_iota(jnp.int32, (ROWS, LANES), 1)
    row = lax.broadcasted_iota(jnp.int32, (ROWS, LANES), 0)
    inside = (lane >= R) & (lane < block_y - R)

    def present(dx, dy):
        return jnp.logical_and(has[dx][0], has[dy][1])

    def landing(dx, dy):
        if dy == 0:
            return from_x.at[(dx + 1) // 2, W]
        if dx == 0:
            return from_y.at[(dy + 1) // 2]
        return from_xy.at[(dx + 1) // 2, (dy + 1) // 2]

    def main_copy(dx):
        first = 0 if dx < 0 else block_x
        return pltpu.make_async_remote_copy(
            src_ref=send.at[pl.ds(first, W)],
            dst_ref=from_x.at[(1 - dx) // 2, pl.ds(0, W)],
            send_sem=send_main.at[(dx + 1) // 2],
            recv_sem=recv_main.at[(1 - dx) // 2],
            device_id=(gx + dx, gy),
            device_id_type=MESH,
        )

    def rim_copy(k, dx, dy):
        return pltpu.make_async_remote_copy(
            src_ref=send.at[span_x],
            dst_ref=landing(-dx, -dy),
            send_sem=send_rim.at[k],
            recv_sem=recv_rim.at[len(others) - 1 - k],
            device_id=(gx + dx, gy + dy),
            device_id_type=MESH,
        )

    def main_arrival(dx):
        return pltpu.make_async_remote_copy(
            src_ref=send.at[pl.ds(0, W)],
            dst_ref=from_x.at[(dx + 1) // 2, pl.ds(0, W)],
            send_sem=send_main.at[(dx + 1) // 2],
            recv_sem=recv_main.at[(dx + 1) // 2],
            device_id=(gx + dx, gy),
            device_id_type=MESH,
        )

    def rim_arrival(k, dx, dy):
        return pltpu.make_async_remote_copy(
            src_ref=send.at[span_x],
            dst_ref=landing(dx, dy),
            send_sem=send_rim.at[k],
            recv_sem=recv_rim.at[k],
            device_id=(gx + dx, gy + dy),
            device_id_type=MESH,
        )

    def masked(local_x, pairs, value):
        parts = []
        for pair in pairs:
            keep = jnp.broadcast_to(local_x // 2 == pair, (16, chunk))
            keep = jnp.where(keep, 1.0, 0.0).astype(BF)
            parts.append(value * jnp.concatenate([keep] * (2 * ROWS // 16), 0))
        return jnp.concatenate(parts, 0)

    def accumulate(total, left, right):
        total[...] += lax.dot_general(
            left, right, (((1,), (1,)), ((), ())), preferred_element_type=F32
        )

    def tile(pair, parity):
        at = (pair % (span_x // 4)) * 2 * ROWS
        cols = slice(parity * block_y, (parity + 1) * block_y)
        return acc[at : at + ROWS, cols] + acc[at + ROWS : at + 2 * ROWS, cols]

    def ready(first, last):
        for t in range(first, last):
            value = tile(t // 2, t % 2)
            if R <= t < R + block_x:
                value = value + jnp.where(inside, prior[t - R], 0.0)
            send[t] = value

    half = span_x // 4
    barrier = pltpu.get_barrier_semaphore()

    @pl.when(index == 0)
    def _():
        for dx, dy in others:
            @pl.when(present(dx, dy))
            def _():
                pl.semaphore_signal(
                    barrier, inc=1, device_id=(gx + dx, gy + dy), device_id_type=MESH
                )
        acc[...] = jnp.zeros_like(acc)
        acc_rim[...] = jnp.zeros_like(acc_rim)
        weighted[...] = jnp.zeros_like(weighted)
        prior[...] = jnp.zeros_like(prior)
        for x in range(block_x):
            prior[x, 0:species, :] = prior_weight * les[:, x, :]
            prior[x, species : species + 1, :] = jnp.full((1, block_y), prior_weight, F32)
            prior[x, species + 1 : species + 2, :] = 1.0 - jnp.exp(-rate[x : x + 1, :])
        for dx in (-1, 1):
            @pl.when(jnp.logical_not(has[dx][0]))
            def _():
                from_x[(dx + 1) // 2] = jnp.zeros((W + 1, ROWS, LANES), F32)
        for dx, dy in others:
            if dy != 0:
                @pl.when(jnp.logical_not(present(dx, dy)))
                def _():
                    landing(dx, dy)[...] = jnp.zeros((ROWS, LANES), F32)

    @pl.when(index < steps)
    def _():
        weighted[0:species, :] = comp[...] * mass[...]
        weighted[species : species + 1, :] = mass[...]
        value = weighted[...]
        high = value.astype(BF).astype(F32)
        both = jnp.concatenate([high, value - high], 0).astype(BF)
        split[index] = both
        local_x, inner, rim = positions(cell[...], block_x, block_y)
        column = jnp.where(inner < 0, -1, inner + (local_x % 2) * block_y)
        hot[index] = one_hot(column, 2 * block_y, 2 * block_y)
        hot_rim[...] = one_hot(rim, LANES, LANES)
        accumulate(acc, masked(local_x, range(half), both), hot[index])
        accumulate(acc_rim, both, hot_rim[...])

    @pl.when(index == steps - 1)
    def _():
        ready(0, W)
        rim_sum = acc_rim[0:ROWS, :] + acc_rim[ROWS:, :]
        for x in range(block_x):
            t = x + R
            low_at, high_at = t * W + R, side_size + t * W
            low, high = roll(prior[x], low_at), roll(prior[x], high_at + R)
            rim_sum += jnp.where((lane >= low_at) & (lane < low_at + R), low, 0.0)
            rim_sum += jnp.where((lane >= high_at) & (lane < high_at + R), high, 0.0)
        send[span_x] = rim_sum
        acc[...] = jnp.zeros_like(acc)
        number = (1 + (gx > 0).astype(jnp.int32) + (gx < counts[0] - 1).astype(jnp.int32)) * (
            1 + (gy > 0).astype(jnp.int32) + (gy < counts[1] - 1).astype(jnp.int32)
        ) - 1
        pl.semaphore_wait(barrier, number)

        @pl.when(has[-1][0])
        def _():
            main_copy(-1).start()

        for k, (dx, dy) in enumerate(others):
            @pl.when(present(dx, dy))
            def _():
                rim_copy(k, dx, dy).start()

    @pl.when(index >= steps)
    def _():
        at = index - steps
        local_x, _, _ = positions(cell[...], block_x, block_y)
        accumulate(acc, masked(local_x, range(half, 2 * half), split[at]), hot[at])

    @pl.when(index == 2 * steps - 1)
    def _():
        ready(W, span_x)

        @pl.when(has[1][0])
        def _():
            main_copy(1).start()

        for k, (dx, dy) in enumerate(others):
            @pl.when(present(dx, dy))
            def _():
                rim_arrival(k, dx, dy).wait_recv()

        @pl.when(has[1][0])
        def _():
            main_arrival(1).wait_recv()

        def finish(total, x):
            total_mass = total[species : species + 1, :]
            weight = jnp.where(total_mass > 0.0, total_mass, 1.0)
            weight = jnp.broadcast_to(weight, total.shape)
            value = total / jnp.where(row < species, weight, 1.0)
            table[x] = value
            return value

        low_side = lane < side_size
        place_x = jnp.where(low_side, lane, lane - side_size)
        used = lane < 2 * side_size
        behind = used & (place_x < 2 * R * W)
        ahead = used & (place_x >= block_x * W)
        total = send[span_x]
        for dx, dy in others:
            mask = used if dx == 0 else behind if dx < 0 else ahead
            if dy != 0:
                mask = mask & (low_side if dy < 0 else jnp.logical_not(low_side))
            shift = dx * block_x * W + dy * side_size
            total = total + jnp.where(mask, roll(landing(dx, dy)[...], shift), 0.0)
        rim_value = finish(total, span_x)

        def close(t):
            total = send[t]
            if t < W:
                total = total + from_x[0, t]
            if t >= block_x:
                total = total + from_x[1, t - block_x]
            value = finish(total, t)
            if R <= t < R + block_x:
                low_at, high_at = t * W + R, side_size + t * W
                value = jnp.where(lane < R, roll(rim_value, -low_at), value)
                value = jnp.where(
                    lane >= block_y - R, roll(rim_value, block_y - R - high_at), value
                )
                means[:, t - R, :] = value[0:species]

        for t in range(W, span_x):
            close(t)

        @pl.when(has[-1][0])
        def _():
            main_arrival(-1).wait_recv()

        for t in range(W):
            close(t)
        for k, (dx, dy) in enumerate(others):
            @pl.when(present(dx, dy))
            def _():
                rim_copy(k, dx, dy).wait_send()
        for dx in (-1, 1):
            @pl.when(has[dx][0])
            def _():
                main_copy(dx).wait_send()


def stack_levels(target, plain, matrices):
    species = matrices.shape[1]
    plain[...] = jnp.zeros_like(plain)
    plain[0:species, 0:species] = matrices[2]
    plain[HALF : HALF + NS_MID, 0:NS_MID] = matrices[1, 0:NS_MID, 0:NS_MID]
    base = HALF + NS_MID
    plain[base : base + NS_LOW, 0:NS_LOW] = matrices[0, 0:NS_LOW, 0:NS_LOW]
    high, low = halves(plain[...])
    target[:, 0:HALF] = high
    target[:, HALF : 2 * HALF] = high
    target[:, 2 * HALF :] = low


def react_kernel(
    block_x, block_y, comp, cell, level, table, rate, implicit, out,
    hot, hot_rim, left, left_rim, mixed, plain, left_rate, left_implicit,
):
    species = comp.shape[0]
    span_x = block_x + 2 * R

    @pl.when(pl.program_id(0) == 0)
    def _():
        mixed[...] = jnp.zeros_like(mixed)
        stack_levels(left_rate, plain, rate)
        stack_levels(left_implicit, plain, implicit)
        high, low = halves(table[0:span_x].reshape(span_x * ROWS, block_y))
        left[:, 0:block_y] = high
        left[:, block_y:] = low
        value = table[span_x]
        high = value.astype(BF).astype(F32)
        lane = lax.broadcasted_iota(jnp.int32, value.shape, 1)
        low = roll(value - high, LANES // 2)
        left_rim[0:ROWS, :] = jnp.where(lane < LANES // 2, high, low).astype(BF)

    local_x, inner, rim = positions(cell[...], block_x, block_y)
    once = one_hot(inner, block_y, block_y)
    hot[0:block_y, :] = once
    hot[block_y:, :] = once
    once = one_hot(rim, LANES // 2, LANES // 2)
    hot_rim[0 : LANES // 2, :] = once
    hot_rim[LANES // 2 :, :] = once
    rows = jnp.dot(left[...], hot[...], preferred_element_type=F32)
    taken = jnp.dot(left_rim[...], hot_rim[...], preferred_element_type=F32)
    taken = jnp.where(inner < 0, taken, 0.0)
    place = jnp.where(inner < 0, -1, local_x)
    for x in range(span_x):
        taken = jnp.where(place == x, rows[x * ROWS : (x + 1) * ROWS], taken)
    factor = taken[species + 1 : species + 2]
    comp_value = comp[...]
    mixed[0:species, :] = comp_value - factor * (comp_value - taken[0:species])
    levels = level[...]
    full, middle = levels == 2, levels == 1
    high, low = halves(mixed[...])
    right = jnp.concatenate([high, low, high], 0)
    drive = jnp.dot(left_rate[...], right, preferred_element_type=F32)
    base = HALF + NS_MID
    top = jnp.where(
        full, drive[0:NS_MID],
        jnp.where(middle, drive[HALF:base], drive[base : base + NS_MID]),
    )
    source = jnp.tanh(jnp.concatenate([top, drive[NS_MID:HALF]], 0))
    high, low = halves(source)
    right = jnp.concatenate([high, low, high], 0)
    change = jnp.dot(left_implicit[...], right, preferred_element_type=F32)
    top = jnp.where(
        full, change[0:NS_MID],
        jnp.where(middle, change[HALF:base], change[base : base + NS_MID]),
    )
    rest = jnp.where(full, change[NS_MID:species], 0.0)
    out[0:NS_MID, :] = mixed[0:NS_MID, :] + chem_step * top
    out[NS_MID:, :] = mixed[NS_MID:species, :] + chem_step * rest


def per_device(
    counts, composition, particle_mass, particle_cell, particle_level,
    les_mean, mix_rate, rate_matrix, implicit_map,
):
    species, particles = composition.shape
    block_x, block_y = les_mean.shape[1], les_mean.shape[2]
    span_x = block_x + 2 * R
    whole = pl.BlockSpec(memory_space=pltpu.VMEM)
    chunk = 2048
    steps = particles // chunk
    left_rows = span_x // 4 * 2 * ROWS

    def first_pass(rows):
        return pl.BlockSpec((rows, chunk), lambda i: (0, jnp.minimum(i, steps - 1)))

    dma = pltpu.SemaphoreType.DMA
    tiles = (span_x + 1, ROWS, LANES)
    table, means = pl.pallas_call(
        functools.partial(sums_kernel, counts, steps, chunk, block_x, block_y),
        grid=(2 * steps,),
        out_shape=(
            jax.ShapeDtypeStruct(tiles, F32),
            jax.ShapeDtypeStruct(les_mean.shape, F32),
        ),
        in_specs=[
            first_pass(species),
            first_pass(1),
            pl.BlockSpec((2, chunk), lambda i: (0, i % steps)),
            pl.BlockSpec(les_mean.shape, lambda i: (0, 0, 0)),
            pl.BlockSpec(mix_rate.shape, lambda i: (0, 0)),
        ],
        out_specs=(
            pl.BlockSpec(tiles, lambda i: (0, 0, 0)),
            pl.BlockSpec(les_mean.shape, lambda i: (0, 0, 0)),
        ),
        scratch_shapes=[
            pltpu.VMEM((steps, 2 * block_y, chunk), BF),
            pltpu.VMEM((LANES, chunk), BF),
            pltpu.VMEM((ROWS, chunk), F32),
            pltpu.VMEM((steps, 2 * ROWS, chunk), BF),
            pltpu.VMEM((left_rows, 2 * block_y), F32),
            pltpu.VMEM((2 * ROWS, LANES), F32),
            pltpu.VMEM(tiles, F32),
            pltpu.VMEM((block_x, ROWS, block_y), F32),
            pltpu.VMEM((2, W + 1, ROWS, LANES), F32),
            pltpu.VMEM((2, ROWS, LANES), F32),
            pltpu.VMEM((2, 2, ROWS, LANES), F32),
            dma((2,)), dma((2,)), dma((8,)), dma((8,)),
        ],
        compiler_params=pltpu.CompilerParams(
            collective_id=0, has_side_effects=True, vmem_limit_bytes=60 << 20
        ),
    )(composition, particle_mass[None], particle_cell, les_mean, mix_rate)
    stacked = HALF + 2 * NS_MID
    chunk = 1024

    def by_chunk(rows):
        return pl.BlockSpec((rows, chunk), lambda i: (0, i))

    updated = pl.pallas_call(
        functools.partial(react_kernel, block_x, block_y),
        grid=(particles // chunk,),
        out_shape=jax.ShapeDtypeStruct(composition.shape, F32),
        in_specs=[by_chunk(species), by_chunk(2), by_chunk(1), whole, whole, whole],
        out_specs=by_chunk(species),
        scratch_shapes=[
            pltpu.VMEM((2 * block_y, chunk), BF),
            pltpu.VMEM((LANES, chunk), BF),
            pltpu.VMEM((span_x * ROWS, 2 * block_y), BF),
            pltpu.VMEM((ROWS, LANES), BF),
            pltpu.VMEM((HALF, chunk), F32),
            pltpu.VMEM((stacked, HALF), F32),
            pltpu.VMEM((stacked, 3 * HALF), BF),
            pltpu.VMEM((stacked, 3 * HALF), BF),
        ],
        compiler_params=pltpu.CompilerParams(vmem_limit_bytes=48 << 20),
    )(composition, particle_cell, particle_level[None], table, rate_matrix, implicit_map)
    return updated, means


def solution(mesh):
    placed = (
        P(None, ("gx", "gy")),
        P(("gx", "gy")),
        P(None, ("gx", "gy")),
        P(("gx", "gy")),
        P(None, "gx", "gy"),
        P("gx", "gy"),
        P(),
        P(),
    )
    return jax.shard_map(
        functools.partial(per_device, (mesh.shape["gx"], mesh.shape["gy"])),
        mesh=mesh,
        in_specs=placed,
        out_specs=(P(None, ("gx", "gy")), P(None, "gx", "gy")),
        check_vma=False,
    )
```

```python
import functools

import jax
import jax.numpy as jnp
from jax import lax
from jax.experimental import pallas as pl
from jax.experimental.pallas import tpu as pltpu
from jax.sharding import PartitionSpec as P

NS_LOW = 21
NS_MID = 24
R = 2
W = 2 * R
HALF = 64
ROWS = 56
LANES = 128

prior_weight = 16.0
chem_step = 0.5
BF = jnp.bfloat16
F32 = jnp.float32
MESH = pl.DeviceIdType.MESH


def halves(value):
    high = value.astype(BF)
    return high, (value - high.astype(F32)).astype(BF)


def roll(value, shift):
    return pltpu.roll(value, shift % value.shape[1], 1)


def positions(cell, block_x, block_y):
    local_x = cell[0:1] - (lax.axis_index("gx") * block_x - R)
    local_y = cell[1:2] - (lax.axis_index("gy") * block_y - R)
    low_rim = local_y < W
    on_rim = low_rim | (local_y >= block_y)
    rim = jnp.where(low_rim, local_y, local_y - block_y + (block_x + 2 * R) * W) + local_x * W
    return local_x, jnp.where(on_rim, -1, local_y - R), jnp.where(on_rim, rim, -1)


def one_hot(place, rows):
    sub = lax.broadcasted_iota(jnp.int32, (rows, place.shape[1]), 0)
    same = sub.astype(F32).astype(BF) == jnp.broadcast_to(
        place.astype(F32), (rows, place.shape[1])
    ).astype(BF)
    return jnp.where(same, jnp.ones((), BF), jnp.zeros((), BF))


def sums_kernel(
    counts, steps, chunk, block_x, block_y, comp, mass, cell, les, rate, table,
    hot, hot_rim, weighted, split, acc, acc_rim,
    send, prior, from_x, from_y, from_xy, send_main, recv_main, send_rim, recv_rim,
):
    species = comp.shape[0]
    span_x = block_x + 2 * R
    side_size = span_x * W
    gx, gy = lax.axis_index("gx"), lax.axis_index("gy")
    index = pl.program_id(0)
    has = {
        -1: (gx > 0, gy > 0),
        1: (gx < counts[0] - 1, gy < counts[1] - 1),
        0: (True, True),
    }
    others = [(dx, dy) for dx in (-1, 0, 1) for dy in (-1, 0, 1) if (dx, dy) != (0, 0)]
    lane = lax.broadcasted_iota(jnp.int32, (ROWS, LANES), 1)
    row = lax.broadcasted_iota(jnp.int32, (ROWS, LANES), 0)
    inside = (lane >= R) & (lane < block_y - R)

    def present(dx, dy):
        return jnp.logical_and(has[dx][0], has[dy][1])

    def landing(dx, dy):
        if dy == 0:
            return from_x.at[(dx + 1) // 2, W]
        if dx == 0:
            return from_y.at[(dy + 1) // 2]
        return from_xy.at[(dx + 1) // 2, (dy + 1) // 2]

    def main_copy(dx):
        first = 0 if dx < 0 else block_x
        return pltpu.make_async_remote_copy(
            src_ref=send.at[pl.ds(first, W)],
            dst_ref=from_x.at[(1 - dx) // 2, pl.ds(0, W)],
            send_sem=send_main.at[(dx + 1) // 2],
            recv_sem=recv_main.at[(1 - dx) // 2],
            device_id=(gx + dx, gy),
            device_id_type=MESH,
        )

    def rim_copy(k, dx, dy):
        return pltpu.make_async_remote_copy(
            src_ref=send.at[span_x],
            dst_ref=landing(-dx, -dy),
            send_sem=send_rim.at[k],
            recv_sem=recv_rim.at[len(others) - 1 - k],
            device_id=(gx + dx, gy + dy),
            device_id_type=MESH,
        )

    def main_arrival(dx):
        return pltpu.make_async_remote_copy(
            src_ref=send.at[pl.ds(0, W)],
            dst_ref=from_x.at[(dx + 1) // 2, pl.ds(0, W)],
            send_sem=send_main.at[(dx + 1) // 2],
            recv_sem=recv_main.at[(dx + 1) // 2],
            device_id=(gx + dx, gy),
            device_id_type=MESH,
        )

    def rim_arrival(k, dx, dy):
        return pltpu.make_async_remote_copy(
            src_ref=send.at[span_x],
            dst_ref=landing(dx, dy),
            send_sem=send_rim.at[k],
            recv_sem=recv_rim.at[k],
            device_id=(gx + dx, gy + dy),
            device_id_type=MESH,
        )

    def masked(local_x, pairs, value):
        parts = []
        for pair in pairs:
            keep = jnp.broadcast_to(local_x // 2 == pair, (16, chunk))
            keep = jnp.where(keep, 1.0, 0.0).astype(BF)
            parts.append(value * jnp.concatenate([keep] * (2 * ROWS // 16), 0))
        return jnp.concatenate(parts, 0)

    def accumulate(total, left, right):
        total[...] += lax.dot_general(
            left, right, (((1,), (1,)), ((), ())), preferred_element_type=F32
        )

    def tile(pair, parity):
        at = (pair % (span_x // 4)) * 2 * ROWS
        cols = slice(parity * block_y, (parity + 1) * block_y)
        return acc[at : at + ROWS, cols] + acc[at + ROWS : at + 2 * ROWS, cols]

    def ready(first, last):
        for t in range(first, last):
            value = tile(t // 2, t % 2)
            if R <= t < R + block_x:
                value = value + jnp.where(inside, prior[t - R], 0.0)
            send[t] = value

    half = span_x // 4
    barrier = pltpu.get_barrier_semaphore()

    @pl.when(index == 0)
    def _():
        for dx, dy in others:
            @pl.when(present(dx, dy))
            def _():
                pl.semaphore_signal(
                    barrier, inc=1, device_id=(gx + dx, gy + dy), device_id_type=MESH
                )
        acc[...] = jnp.zeros_like(acc)
        acc_rim[...] = jnp.zeros_like(acc_rim)
        weighted[...] = jnp.zeros_like(weighted)
        prior[...] = jnp.zeros_like(prior)
        for x in range(block_x):
            prior[x, 0:species, :] = prior_weight * les[:, x, :]
            prior[x, species : species + 1, :] = jnp.full((1, block_y), prior_weight, F32)
            prior[x, species + 1 : species + 2, :] = 1.0 - jnp.exp(-rate[x : x + 1, :])
        for dx in (-1, 1):
            @pl.when(jnp.logical_not(has[dx][0]))
            def _():
                from_x[(dx + 1) // 2] = jnp.zeros((W + 1, ROWS, LANES), F32)
        for dx, dy in others:
            if dy != 0:
                @pl.when(jnp.logical_not(present(dx, dy)))
                def _():
                    landing(dx, dy)[...] = jnp.zeros((ROWS, LANES), F32)

    @pl.when(index < steps)
    def _():
        weighted[0:species, :] = comp[...] * mass[...]
        weighted[species : species + 1, :] = mass[...]
        value = weighted[...]
        high = value.astype(BF).astype(F32)
        both = jnp.concatenate([high, value - high], 0).astype(BF)
        split[index] = both
        local_x, inner, rim = positions(cell[...], block_x, block_y)
        column = jnp.where(inner < 0, -1, inner + (local_x % 2) * block_y)
        hot[index] = one_hot(column, 2 * block_y)
        hot_rim[...] = one_hot(rim, HALF)
        accumulate(acc, masked(local_x, range(half), both), hot[index])
        acc_rim[:, 0:HALF] += lax.dot_general(
            both, hot_rim[...], (((1,), (1,)), ((), ())), preferred_element_type=F32
        )

    @pl.when(index == steps - 1)
    def _():
        ready(0, W)
        rim_sum = acc_rim[0:ROWS, :] + acc_rim[ROWS:, :]
        for x in range(block_x):
            t = x + R
            low_at, high_at = t * W + R, side_size + t * W
            low, high = roll(prior[x], low_at), roll(prior[x], high_at + R)
            rim_sum += jnp.where((lane >= low_at) & (lane < low_at + R), low, 0.0)
            rim_sum += jnp.where((lane >= high_at) & (lane < high_at + R), high, 0.0)
        send[span_x] = rim_sum
        acc[...] = jnp.zeros_like(acc)
        number = (1 + (gx > 0).astype(jnp.int32) + (gx < counts[0] - 1).astype(jnp.int32)) * (
            1 + (gy > 0).astype(jnp.int32) + (gy < counts[1] - 1).astype(jnp.int32)
        ) - 1
        pl.semaphore_wait(barrier, number)

        @pl.when(has[-1][0])
        def _():
            main_copy(-1).start()

        for k, (dx, dy) in enumerate(others):
            @pl.when(present(dx, dy))
            def _():
                rim_copy(k, dx, dy).start()

    @pl.when(index >= steps)
    def _():
        at = index - steps
        local_x, _, _ = positions(cell[...], block_x, block_y)
        accumulate(acc, masked(local_x, range(half, 2 * half), split[at]), hot[at])

    @pl.when(index == 2 * steps - 1)
    def _():
        ready(W, span_x)

        @pl.when(has[1][0])
        def _():
            main_copy(1).start()

        for k, (dx, dy) in enumerate(others):
            @pl.when(present(dx, dy))
            def _():
                rim_arrival(k, dx, dy).wait_recv()

        @pl.when(has[1][0])
        def _():
            main_arrival(1).wait_recv()

        def finish(total):
            total_mass = total[species : species + 1, :]
            weight = jnp.where(total_mass > 0.0, total_mass, 1.0)
            weight = jnp.broadcast_to(weight, total.shape)
            return total / jnp.where(row < species, weight, 1.0)

        low_side = lane < side_size
        place_x = jnp.where(low_side, lane, lane - side_size)
        used = lane < 2 * side_size
        behind = used & (place_x < 2 * R * W)
        ahead = used & (place_x >= block_x * W)
        total = send[span_x]
        for dx, dy in others:
            mask = used if dx == 0 else behind if dx < 0 else ahead
            if dy != 0:
                mask = mask & (low_side if dy < 0 else jnp.logical_not(low_side))
            shift = dx * block_x * W + dy * side_size
            total = total + jnp.where(mask, roll(landing(dx, dy)[...], shift), 0.0)
        rim_value = finish(total)
        table[span_x] = rim_value

        def close(t):
            total = send[t]
            if t < W:
                total = total + from_x[0, t]
            if t >= block_x:
                total = total + from_x[1, t - block_x]
            value = finish(total)
            if R <= t < R + block_x:
                low_at, high_at = t * W + R, side_size + t * W
                value = jnp.where(lane < R, roll(rim_value, -low_at), value)
                value = jnp.where(
                    lane >= block_y - R, roll(rim_value, block_y - R - high_at), value
                )
            table[t] = value

        for t in range(W, span_x):
            close(t)

        @pl.when(has[-1][0])
        def _():
            main_arrival(-1).wait_recv()

        for t in range(W):
            close(t)
        for k, (dx, dy) in enumerate(others):
            @pl.when(present(dx, dy))
            def _():
                rim_copy(k, dx, dy).wait_send()
        for dx in (-1, 1):
            @pl.when(has[dx][0])
            def _():
                main_copy(dx).wait_send()


def stack_levels(target, plain, matrices):
    species = matrices.shape[1]
    plain[...] = jnp.zeros_like(plain)
    plain[0:species, 0:species] = matrices[2]
    plain[HALF : HALF + NS_MID, 0:NS_MID] = matrices[1, 0:NS_MID, 0:NS_MID]
    base = HALF + NS_MID
    plain[base : base + NS_LOW, 0:NS_LOW] = matrices[0, 0:NS_LOW, 0:NS_LOW]
    high, low = halves(plain[...])
    target[:, 0:HALF] = high
    target[:, HALF : 2 * HALF] = high
    target[:, 2 * HALF :] = low


def react_kernel(
    block_x, block_y, comp, cell, level, table, rate, implicit, out, means,
    left, left_rim, mixed, plain, left_rate, left_implicit,
):
    species = comp.shape[0]
    span_x = block_x + 2 * R
    piece = 256

    @pl.when(pl.program_id(0) == 0)
    def _():
        mixed[...] = jnp.zeros_like(mixed)
        stack_levels(left_rate, plain, rate)
        stack_levels(left_implicit, plain, implicit)
        high, low = halves(table[0:span_x].reshape(span_x * ROWS, block_y))
        left[:, 0:block_y] = high
        left[:, block_y:] = low
        value = table[span_x]
        high = value.astype(BF).astype(F32)
        lane = lax.broadcasted_iota(jnp.int32, value.shape, 1)
        low = roll(value - high, HALF)
        left_rim[...] = jnp.where(lane < HALF, high, low).astype(BF)
        for x in range(block_x):
            means[:, x, :] = table[x + R, 0:species, :]

    def choose(test, yes, no):
        shape = (yes.shape[0] // 8, 8, piece)
        return jnp.where(test[None], yes.reshape(shape), no.reshape(shape)).reshape(yes.shape)

    def work(at):
        span = slice(at, at + piece)
        local_x, inner, rim = positions(cell[:, span], block_x, block_y)
        hot = one_hot(inner, block_y)
        hot_rim = one_hot(rim, HALF)
        rows = jnp.dot(left[...], jnp.concatenate([hot, hot], 0), preferred_element_type=F32)
        on_rim = jnp.dot(
            left_rim[...], jnp.concatenate([hot_rim, hot_rim], 0), preferred_element_type=F32
        )
        place = jnp.broadcast_to(local_x, (8, piece))
        parts = [rows[x * ROWS : (x + 1) * ROWS] for x in range(span_x)]
        bit = 1
        while len(parts) > 1:
            test = (place & bit) != 0
            paired = [
                choose(test, parts[i + 1], parts[i]) for i in range(0, len(parts) - 1, 2)
            ]
            parts = paired + parts[2 * len(paired) :]
            bit *= 2
        taken = choose(jnp.broadcast_to(inner, (8, piece)) < 0, on_rim, parts[0])
        factor = taken[species + 1 : species + 2]
        comp_value = comp[:, span]
        mixed[0:species, span] = comp_value - factor * (comp_value - taken[0:species])
        levels = jnp.broadcast_to(level[:, span], (8, piece))
        full, middle = levels == 2, levels == 1
        base = HALF + NS_MID

        def pick(value):
            return choose(
                full, value[0:NS_MID],
                choose(middle, value[HALF:base], value[base : base + NS_MID]),
            )

        high, low = halves(mixed[:, span])
        right = jnp.concatenate([high, low, high], 0)
        drive = jnp.dot(left_rate[...], right, preferred_element_type=F32)
        source = jnp.tanh(jnp.concatenate([pick(drive), drive[NS_MID:HALF]], 0))
        high, low = halves(source)
        right = jnp.concatenate([high, low, high], 0)
        change = jnp.dot(left_implicit[...], right, preferred_element_type=F32)
        rest = change[NS_MID:ROWS]
        rest = choose(full, rest, jnp.zeros_like(rest))
        out[0:NS_MID, span] = mixed[0:NS_MID, span] + chem_step * pick(change)
        out[NS_MID:, span] = mixed[NS_MID:species, span] + chem_step * rest[0 : species - NS_MID]

    for at in range(0, comp.shape[1], piece):
        work(at)


def per_device(
    counts, composition, particle_mass, particle_cell, particle_level,
    les_mean, mix_rate, rate_matrix, implicit_map,
):
    species, particles = composition.shape
    block_x, block_y = les_mean.shape[1], les_mean.shape[2]
    span_x = block_x + 2 * R
    whole = pl.BlockSpec(memory_space=pltpu.VMEM)
    chunk = 2048
    steps = particles // chunk
    left_rows = span_x // 4 * 2 * ROWS

    def first_pass(rows):
        return pl.BlockSpec((rows, chunk), lambda i: (0, jnp.minimum(i, steps - 1)))

    dma = pltpu.SemaphoreType.DMA
    tiles = (span_x + 1, ROWS, LANES)
    table = pl.pallas_call(
        functools.partial(sums_kernel, counts, steps, chunk, block_x, block_y),
        grid=(2 * steps,),
        out_shape=jax.ShapeDtypeStruct(tiles, F32),
        in_specs=[
            first_pass(species),
            first_pass(1),
            pl.BlockSpec((2, chunk), lambda i: (0, i % steps)),
            pl.BlockSpec(les_mean.shape, lambda i: (0, 0, 0)),
            pl.BlockSpec(mix_rate.shape, lambda i: (0, 0)),
        ],
        out_specs=pl.BlockSpec(tiles, lambda i: (0, 0, 0)),
        scratch_shapes=[
            pltpu.VMEM((steps, 2 * block_y, chunk), BF),
            pltpu.VMEM((HALF, chunk), BF),
            pltpu.VMEM((ROWS, chunk), F32),
            pltpu.VMEM((steps, 2 * ROWS, chunk), BF),
            pltpu.VMEM((left_rows, 2 * block_y), F32),
            pltpu.VMEM((2 * ROWS, LANES), F32),
            pltpu.VMEM(tiles, F32),
            pltpu.VMEM((block_x, ROWS, block_y), F32),
            pltpu.VMEM((2, W + 1, ROWS, LANES), F32),
            pltpu.VMEM((2, ROWS, LANES), F32),
            pltpu.VMEM((2, 2, ROWS, LANES), F32),
            dma((2,)), dma((2,)), dma((8,)), dma((8,)),
        ],
        compiler_params=pltpu.CompilerParams(
            collective_id=0, has_side_effects=True, vmem_limit_bytes=60 << 20
        ),
    )(composition, particle_mass[None], particle_cell, les_mean, mix_rate)
    stacked = HALF + 2 * NS_MID
    chunk = 1024

    def by_chunk(rows):
        return pl.BlockSpec((rows, chunk), lambda i: (0, i))

    def fixed(array):
        return pl.BlockSpec(array.shape, lambda i: (0,) * array.ndim)

    return pl.pallas_call(
        functools.partial(react_kernel, block_x, block_y),
        grid=(particles // chunk,),
        out_shape=(
            jax.ShapeDtypeStruct(composition.shape, F32),
            jax.ShapeDtypeStruct(les_mean.shape, F32),
        ),
        in_specs=[
            by_chunk(species), by_chunk(2), by_chunk(1),
            fixed(table), fixed(rate_matrix), fixed(implicit_map),
        ],
        out_specs=(by_chunk(species), fixed(les_mean)),
        scratch_shapes=[
            pltpu.VMEM((span_x * ROWS, 2 * block_y), BF),
            pltpu.VMEM((ROWS, LANES), BF),
            pltpu.VMEM((HALF, chunk), F32),
            pltpu.VMEM((stacked, HALF), F32),
            pltpu.VMEM((stacked, 3 * HALF), BF),
            pltpu.VMEM((stacked, 3 * HALF), BF),
        ],
        compiler_params=pltpu.CompilerParams(vmem_limit_bytes=60 << 20),
    )(composition, particle_cell, particle_level[None], table, rate_matrix, implicit_map)


def solution(mesh):
    placed = (
        P(None, ("gx", "gy")),
        P(("gx", "gy")),
        P(None, ("gx", "gy")),
        P(("gx", "gy")),
        P(None, "gx", "gy"),
        P("gx", "gy"),
        P(),
        P(),
    )
    return jax.shard_map(
        functools.partial(per_device, (mesh.shape["gx"], mesh.shape["gy"])),
        mesh=mesh,
        in_specs=placed,
        out_specs=(P(None, ("gx", "gy")), P(None, "gx", "gy")),
        check_vma=False,
    )
```

```python
import functools

import jax
import jax.numpy as jnp
from jax import lax
from jax.experimental import pallas as pl
from jax.experimental.pallas import tpu as pltpu
from jax.sharding import PartitionSpec as P

NS_LOW = 21
NS_MID = 24
R = 2
W = 2 * R
HALF = 64
ROWS = 56
LANES = 128

prior_weight = 16.0
chem_step = 0.5
BF = jnp.bfloat16
F32 = jnp.float32
MESH = pl.DeviceIdType.MESH


def halves(value):
    high = value.astype(BF)
    return high, (value - high.astype(F32)).astype(BF)


def roll(value, shift):
    return pltpu.roll(value, shift % value.shape[1], 1)


def positions(cell, block_x, block_y):
    local_x = cell[0:1] - (lax.axis_index("gx") * block_x - R)
    local_y = cell[1:2] - (lax.axis_index("gy") * block_y - R)
    low_rim = local_y < W
    on_rim = low_rim | (local_y >= block_y)
    rim = jnp.where(low_rim, local_y, local_y - block_y + (block_x + 2 * R) * W) + local_x * W
    return local_x, jnp.where(on_rim, -1, local_y - R), jnp.where(on_rim, rim, -1)


def one_hot(place, rows):
    sub = lax.broadcasted_iota(jnp.int32, (rows, place.shape[1]), 0)
    same = sub.astype(F32).astype(BF) == jnp.broadcast_to(
        place.astype(F32), (rows, place.shape[1])
    ).astype(BF)
    return jnp.where(same, jnp.ones((), BF), jnp.zeros((), BF))


def sums_kernel(
    counts, steps, chunk, block_x, block_y, comp, mass, cell, les, rate, table,
    hot, hot_rim, weighted, split, acc, acc_rim,
    send, prior, from_x, from_y, from_xy, send_main, recv_main, send_rim, recv_rim,
):
    species = comp.shape[0]
    span_x = block_x + 2 * R
    side_size = span_x * W
    gx, gy = lax.axis_index("gx"), lax.axis_index("gy")
    index = pl.program_id(0)
    has = {
        -1: (gx > 0, gy > 0),
        1: (gx < counts[0] - 1, gy < counts[1] - 1),
        0: (True, True),
    }
    others = [(dx, dy) for dx in (-1, 0, 1) for dy in (-1, 0, 1) if (dx, dy) != (0, 0)]
    lane = lax.broadcasted_iota(jnp.int32, (ROWS, LANES), 1)
    row = lax.broadcasted_iota(jnp.int32, (ROWS, LANES), 0)
    inside = (lane >= R) & (lane < block_y - R)

    def present(dx, dy):
        return jnp.logical_and(has[dx][0], has[dy][1])

    def landing(dx, dy):
        if dy == 0:
            return from_x.at[(dx + 1) // 2, W]
        if dx == 0:
            return from_y.at[(dy + 1) // 2]
        return from_xy.at[(dx + 1) // 2, (dy + 1) // 2]

    def main_copy(dx):
        first = 0 if dx < 0 else block_x
        return pltpu.make_async_remote_copy(
            src_ref=send.at[pl.ds(first, W)],
            dst_ref=from_x.at[(1 - dx) // 2, pl.ds(0, W)],
            send_sem=send_main.at[(dx + 1) // 2],
            recv_sem=recv_main.at[(1 - dx) // 2],
            device_id=(gx + dx, gy),
            device_id_type=MESH,
        )

    def rim_copy(k, dx, dy):
        return pltpu.make_async_remote_copy(
            src_ref=send.at[span_x],
            dst_ref=landing(-dx, -dy),
            send_sem=send_rim.at[k],
            recv_sem=recv_rim.at[len(others) - 1 - k],
            device_id=(gx + dx, gy + dy),
            device_id_type=MESH,
        )

    def main_arrival(dx):
        return pltpu.make_async_remote_copy(
            src_ref=send.at[pl.ds(0, W)],
            dst_ref=from_x.at[(dx + 1) // 2, pl.ds(0, W)],
            send_sem=send_main.at[(dx + 1) // 2],
            recv_sem=recv_main.at[(dx + 1) // 2],
            device_id=(gx + dx, gy),
            device_id_type=MESH,
        )

    def rim_arrival(k, dx, dy):
        return pltpu.make_async_remote_copy(
            src_ref=send.at[span_x],
            dst_ref=landing(dx, dy),
            send_sem=send_rim.at[k],
            recv_sem=recv_rim.at[k],
            device_id=(gx + dx, gy + dy),
            device_id_type=MESH,
        )

    def masked(local_x, pairs, value):
        parts = []
        for pair in pairs:
            keep = jnp.broadcast_to(local_x // 2 == pair, (16, chunk))
            keep = jnp.where(keep, 1.0, 0.0).astype(BF)
            parts.append(value * jnp.concatenate([keep] * (2 * ROWS // 16), 0))
        return jnp.concatenate(parts, 0)

    def accumulate(total, left, right):
        total[...] += lax.dot_general(
            left, right, (((1,), (1,)), ((), ())), preferred_element_type=F32
        )

    def tile(pair, parity):
        at = (pair % (span_x // 4)) * 2 * ROWS
        cols = slice(parity * block_y, (parity + 1) * block_y)
        return acc[at : at + ROWS, cols] + acc[at + ROWS : at + 2 * ROWS, cols]

    def ready(first, last):
        for t in range(first, last):
            value = tile(t // 2, t % 2)
            if R <= t < R + block_x:
                value = value + jnp.where(inside, prior[t - R], 0.0)
            send[t] = value

    half = span_x // 4
    barrier = pltpu.get_barrier_semaphore()

    @pl.when(index == 0)
    def _():
        for dx, dy in others:
            @pl.when(present(dx, dy))
            def _():
                pl.semaphore_signal(
                    barrier, inc=1, device_id=(gx + dx, gy + dy), device_id_type=MESH
                )
        acc[...] = jnp.zeros_like(acc)
        acc_rim[...] = jnp.zeros_like(acc_rim)
        weighted[...] = jnp.zeros_like(weighted)
        prior[...] = jnp.zeros_like(prior)
        for x in range(block_x):
            prior[x, 0:species, :] = prior_weight * les[:, x, :]
            prior[x, species : species + 1, :] = jnp.full((1, block_y), prior_weight, F32)
            prior[x, species + 1 : species + 2, :] = 1.0 - jnp.exp(-rate[x : x + 1, :])
        for dx in (-1, 1):
            @pl.when(jnp.logical_not(has[dx][0]))
            def _():
                from_x[(dx + 1) // 2] = jnp.zeros((W + 1, ROWS, LANES), F32)
        for dx, dy in others:
            if dy != 0:
                @pl.when(jnp.logical_not(present(dx, dy)))
                def _():
                    landing(dx, dy)[...] = jnp.zeros((ROWS, LANES), F32)

    @pl.when(index < steps)
    def _():
        weighted[0:species, :] = comp[...] * mass[...]
        weighted[species : species + 1, :] = mass[...]
        value = weighted[...]
        high = value.astype(BF).astype(F32)
        both = jnp.concatenate([high, value - high], 0).astype(BF)
        split[index] = both
        local_x, inner, rim = positions(cell[...], block_x, block_y)
        column = jnp.where(inner < 0, -1, inner + (local_x % 2) * block_y)
        hot[index] = one_hot(column, 2 * block_y)
        hot_rim[...] = one_hot(rim, HALF)
        accumulate(acc, masked(local_x, range(half), both), hot[index])
        acc_rim[:, 0:HALF] += lax.dot_general(
            both, hot_rim[...], (((1,), (1,)), ((), ())), preferred_element_type=F32
        )

    @pl.when(index == steps - 1)
    def _():
        ready(0, W)
        rim_sum = acc_rim[0:ROWS, :] + acc_rim[ROWS:, :]
        for x in range(block_x):
            t = x + R
            low_at, high_at = t * W + R, side_size + t * W
            low, high = roll(prior[x], low_at), roll(prior[x], high_at + R)
            rim_sum += jnp.where((lane >= low_at) & (lane < low_at + R), low, 0.0)
            rim_sum += jnp.where((lane >= high_at) & (lane < high_at + R), high, 0.0)
        send[span_x] = rim_sum
        acc[...] = jnp.zeros_like(acc)
        number = (1 + (gx > 0).astype(jnp.int32) + (gx < counts[0] - 1).astype(jnp.int32)) * (
            1 + (gy > 0).astype(jnp.int32) + (gy < counts[1] - 1).astype(jnp.int32)
        ) - 1
        pl.semaphore_wait(barrier, number)

        @pl.when(has[-1][0])
        def _():
            main_copy(-1).start()

        for k, (dx, dy) in enumerate(others):
            @pl.when(present(dx, dy))
            def _():
                rim_copy(k, dx, dy).start()

    @pl.when(index >= steps)
    def _():
        at = index - steps
        local_x, _, _ = positions(cell[...], block_x, block_y)
        accumulate(acc, masked(local_x, range(half, 2 * half), split[at]), hot[at])

    @pl.when(index == 2 * steps - 1)
    def _():
        ready(W, span_x)

        @pl.when(has[1][0])
        def _():
            main_copy(1).start()

        for k, (dx, dy) in enumerate(others):
            @pl.when(present(dx, dy))
            def _():
                rim_arrival(k, dx, dy).wait_recv()

        @pl.when(has[1][0])
        def _():
            main_arrival(1).wait_recv()

        def finish(total):
            total_mass = total[species : species + 1, :]
            weight = jnp.where(total_mass > 0.0, total_mass, 1.0)
            weight = jnp.broadcast_to(weight, total.shape)
            return total / jnp.where(row < species, weight, 1.0)

        low_side = lane < side_size
        place_x = jnp.where(low_side, lane, lane - side_size)
        used = lane < 2 * side_size
        behind = used & (place_x < 2 * R * W)
        ahead = used & (place_x >= block_x * W)
        total = send[span_x]
        for dx, dy in others:
            mask = used if dx == 0 else behind if dx < 0 else ahead
            if dy != 0:
                mask = mask & (low_side if dy < 0 else jnp.logical_not(low_side))
            shift = dx * block_x * W + dy * side_size
            total = total + jnp.where(mask, roll(landing(dx, dy)[...], shift), 0.0)
        rim_value = finish(total)
        table[span_x] = rim_value

        def close(t):
            total = send[t]
            if t < W:
                total = total + from_x[0, t]
            if t >= block_x:
                total = total + from_x[1, t - block_x]
            value = finish(total)
            if R <= t < R + block_x:
                low_at, high_at = t * W + R, side_size + t * W
                value = jnp.where(lane < R, roll(rim_value, -low_at), value)
                value = jnp.where(
                    lane >= block_y - R, roll(rim_value, block_y - R - high_at), value
                )
            table[t] = value

        for t in range(W, span_x):
            close(t)

        @pl.when(has[-1][0])
        def _():
            main_arrival(-1).wait_recv()

        for t in range(W):
            close(t)
        for k, (dx, dy) in enumerate(others):
            @pl.when(present(dx, dy))
            def _():
                rim_copy(k, dx, dy).wait_send()
        for dx in (-1, 1):
            @pl.when(has[dx][0])
            def _():
                main_copy(dx).wait_send()


def stack_levels(target, plain, matrices):
    species = matrices.shape[1]
    plain[...] = jnp.zeros_like(plain)
    plain[0:species, 0:species] = matrices[2]
    plain[HALF : HALF + NS_MID, 0:NS_MID] = matrices[1, 0:NS_MID, 0:NS_MID]
    base = HALF + NS_MID
    plain[base : base + NS_LOW, 0:NS_LOW] = matrices[0, 0:NS_LOW, 0:NS_LOW]
    high, low = halves(plain[...])
    target[:, 0:HALF] = high
    target[:, HALF : 2 * HALF] = high
    target[:, 2 * HALF :] = low


def react_kernel(
    block_x, block_y, comp, cell, level, table, rate, implicit, out, means,
    left, left_rim, mixed, plain, left_rate, left_implicit,
):
    species = comp.shape[0]
    span_x = block_x + 2 * R
    piece = 2048

    @pl.when(pl.program_id(0) == 0)
    def _():
        mixed[...] = jnp.zeros_like(mixed)
        stack_levels(left_rate, plain, rate)
        stack_levels(left_implicit, plain, implicit)
        high, low = halves(table[0:span_x].reshape(span_x * ROWS, block_y))
        left[:, 0:block_y] = high
        left[:, block_y:] = low
        value = table[span_x]
        high = value.astype(BF).astype(F32)
        lane = lax.broadcasted_iota(jnp.int32, value.shape, 1)
        low = roll(value - high, HALF)
        left_rim[...] = jnp.where(lane < HALF, high, low).astype(BF)
        for x in range(block_x):
            means[:, x, :] = table[x + R, 0:species, :]

    def choose(test, yes, no):
        shape = (yes.shape[0] // 8, 8, piece)
        return jnp.where(test[None], yes.reshape(shape), no.reshape(shape)).reshape(yes.shape)

    def work(at):
        span = slice(at, at + piece)
        local_x, inner, rim = positions(cell[:, span], block_x, block_y)
        hot = one_hot(inner, block_y)
        hot_rim = one_hot(rim, HALF)
        rows = jnp.dot(left[...], jnp.concatenate([hot, hot], 0), preferred_element_type=F32)
        on_rim = jnp.dot(
            left_rim[...], jnp.concatenate([hot_rim, hot_rim], 0), preferred_element_type=F32
        )
        place = jnp.broadcast_to(local_x, (8, piece))
        parts = [rows[x * ROWS : (x + 1) * ROWS] for x in range(span_x)]
        bit = 1
        while len(parts) > 1:
            test = (place & bit) != 0
            paired = [
                choose(test, parts[i + 1], parts[i]) for i in range(0, len(parts) - 1, 2)
            ]
            parts = paired + parts[2 * len(paired) :]
            bit *= 2
        taken = choose(jnp.broadcast_to(inner, (8, piece)) < 0, on_rim, parts[0])
        factor = taken[species + 1 : species + 2]
        comp_value = comp[:, span]
        mixed[0:species, span] = comp_value - factor * (comp_value - taken[0:species])
        levels = jnp.broadcast_to(level[:, span], (8, piece))
        full, middle = levels == 2, levels == 1
        base = HALF + NS_MID

        def pick(value):
            return choose(
                full, value[0:NS_MID],
                choose(middle, value[HALF:base], value[base : base + NS_MID]),
            )

        high, low = halves(mixed[:, span])
        right = jnp.concatenate([high, low, high], 0)
        drive = jnp.dot(left_rate[...], right, preferred_element_type=F32)
        source = jnp.tanh(jnp.concatenate([pick(drive), drive[NS_MID:HALF]], 0))
        high, low = halves(source)
        right = jnp.concatenate([high, low, high], 0)
        change = jnp.dot(left_implicit[...], right, preferred_element_type=F32)
        rest = change[NS_MID:ROWS]
        rest = choose(full, rest, jnp.zeros_like(rest))
        out[0:NS_MID, span] = mixed[0:NS_MID, span] + chem_step * pick(change)
        out[NS_MID:, span] = mixed[NS_MID:species, span] + chem_step * rest[0 : species - NS_MID]

    for at in range(0, comp.shape[1], piece):
        work(at)


def per_device(
    counts, composition, particle_mass, particle_cell, particle_level,
    les_mean, mix_rate, rate_matrix, implicit_map,
):
    species, particles = composition.shape
    block_x, block_y = les_mean.shape[1], les_mean.shape[2]
    span_x = block_x + 2 * R
    whole = pl.BlockSpec(memory_space=pltpu.VMEM)
    chunk = 2048
    steps = particles // chunk
    left_rows = span_x // 4 * 2 * ROWS

    def first_pass(rows):
        return pl.BlockSpec((rows, chunk), lambda i: (0, jnp.minimum(i, steps - 1)))

    dma = pltpu.SemaphoreType.DMA
    tiles = (span_x + 1, ROWS, LANES)
    table = pl.pallas_call(
        functools.partial(sums_kernel, counts, steps, chunk, block_x, block_y),
        grid=(2 * steps,),
        out_shape=jax.ShapeDtypeStruct(tiles, F32),
        in_specs=[
            first_pass(species),
            first_pass(1),
            pl.BlockSpec((2, chunk), lambda i: (0, i % steps)),
            pl.BlockSpec(les_mean.shape, lambda i: (0, 0, 0)),
            pl.BlockSpec(mix_rate.shape, lambda i: (0, 0)),
        ],
        out_specs=pl.BlockSpec(tiles, lambda i: (0, 0, 0)),
        scratch_shapes=[
            pltpu.VMEM((steps, 2 * block_y, chunk), BF),
            pltpu.VMEM((HALF, chunk), BF),
            pltpu.VMEM((ROWS, chunk), F32),
            pltpu.VMEM((steps, 2 * ROWS, chunk), BF),
            pltpu.VMEM((left_rows, 2 * block_y), F32),
            pltpu.VMEM((2 * ROWS, LANES), F32),
            pltpu.VMEM(tiles, F32),
            pltpu.VMEM((block_x, ROWS, block_y), F32),
            pltpu.VMEM((2, W + 1, ROWS, LANES), F32),
            pltpu.VMEM((2, ROWS, LANES), F32),
            pltpu.VMEM((2, 2, ROWS, LANES), F32),
            dma((2,)), dma((2,)), dma((8,)), dma((8,)),
        ],
        compiler_params=pltpu.CompilerParams(
            collective_id=0, has_side_effects=True, vmem_limit_bytes=60 << 20
        ),
    )(composition, particle_mass[None], particle_cell, les_mean, mix_rate)
    stacked = HALF + 2 * NS_MID
    chunk = 2048

    def by_chunk(rows):
        return pl.BlockSpec((rows, chunk), lambda i: (0, i))

    def fixed(array):
        return pl.BlockSpec(array.shape, lambda i: (0,) * array.ndim)

    return pl.pallas_call(
        functools.partial(react_kernel, block_x, block_y),
        grid=(particles // chunk,),
        out_shape=(
            jax.ShapeDtypeStruct(composition.shape, F32),
            jax.ShapeDtypeStruct(les_mean.shape, F32),
        ),
        in_specs=[
            by_chunk(species), by_chunk(2), by_chunk(1),
            fixed(table), fixed(rate_matrix), fixed(implicit_map),
        ],
        out_specs=(by_chunk(species), fixed(les_mean)),
        scratch_shapes=[
            pltpu.VMEM((span_x * ROWS, 2 * block_y), BF),
            pltpu.VMEM((ROWS, LANES), BF),
            pltpu.VMEM((HALF, chunk), F32),
            pltpu.VMEM((stacked, HALF), F32),
            pltpu.VMEM((stacked, 3 * HALF), BF),
            pltpu.VMEM((stacked, 3 * HALF), BF),
        ],
        compiler_params=pltpu.CompilerParams(vmem_limit_bytes=60 << 20),
    )(composition, particle_cell, particle_level[None], table, rate_matrix, implicit_map)


def solution(mesh):
    placed = (
        P(None, ("gx", "gy")),
        P(("gx", "gy")),
        P(None, ("gx", "gy")),
        P(("gx", "gy")),
        P(None, "gx", "gy"),
        P("gx", "gy"),
        P(),
        P(),
    )
    return jax.shard_map(
        functools.partial(per_device, (mesh.shape["gx"], mesh.shape["gy"])),
        mesh=mesh,
        in_specs=placed,
        out_specs=(P(None, ("gx", "gy")), P(None, "gx", "gy")),
        check_vma=False,
    )
```

```python
import functools

import jax
import jax.numpy as jnp
from jax import lax
from jax.experimental import pallas as pl
from jax.experimental.pallas import tpu as pltpu
from jax.sharding import PartitionSpec as P

NS_LOW = 21
NS_MID = 24
R = 2
W = 2 * R
HALF = 64
ROWS = 56
LANES = 128

prior_weight = 16.0
chem_step = 0.5
BF = jnp.bfloat16
F32 = jnp.float32
MESH = pl.DeviceIdType.MESH


def halves(value):
    high = value.astype(BF)
    return high, (value - high.astype(F32)).astype(BF)


def roll(value, shift):
    return pltpu.roll(value, shift % value.shape[1], 1)


def positions(cell, block_x, block_y):
    local_x = cell[0:1] - (lax.axis_index("gx") * block_x - R)
    local_y = cell[1:2] - (lax.axis_index("gy") * block_y - R)
    low_rim = local_y < W
    on_rim = low_rim | (local_y >= block_y)
    rim = jnp.where(low_rim, local_y, local_y - block_y + (block_x + 2 * R) * W) + local_x * W
    return local_x, jnp.where(on_rim, -1, local_y - R), jnp.where(on_rim, rim, -1)


def one_hot(place, rows):
    sub = lax.broadcasted_iota(jnp.int32, (rows, place.shape[1]), 0)
    same = sub.astype(F32).astype(BF) == jnp.broadcast_to(
        place.astype(F32), (rows, place.shape[1])
    ).astype(BF)
    return jnp.where(same, jnp.ones((), BF), jnp.zeros((), BF))


def sums_kernel(
    counts, steps, chunk, block_x, block_y, comp, mass, cell, les, rate, table,
    hot, hot_rim, weighted, split, acc, acc_rim,
    send, prior, from_x, from_y, from_xy, send_main, recv_main, send_rim, recv_rim,
):
    species = comp.shape[0]
    span_x = block_x + 2 * R
    side_size = span_x * W
    gx, gy = lax.axis_index("gx"), lax.axis_index("gy")
    index = pl.program_id(0)
    has = {
        -1: (gx > 0, gy > 0),
        1: (gx < counts[0] - 1, gy < counts[1] - 1),
        0: (True, True),
    }
    others = [(dx, dy) for dx in (-1, 0, 1) for dy in (-1, 0, 1) if (dx, dy) != (0, 0)]
    lane = lax.broadcasted_iota(jnp.int32, (ROWS, LANES), 1)
    row = lax.broadcasted_iota(jnp.int32, (ROWS, LANES), 0)
    inside = (lane >= R) & (lane < block_y - R)

    def present(dx, dy):
        return jnp.logical_and(has[dx][0], has[dy][1])

    def landing(dx, dy):
        if dy == 0:
            return from_x.at[(dx + 1) // 2, W]
        if dx == 0:
            return from_y.at[(dy + 1) // 2]
        return from_xy.at[(dx + 1) // 2, (dy + 1) // 2]

    def main_copy(dx):
        first = 0 if dx < 0 else block_x
        return pltpu.make_async_remote_copy(
            src_ref=send.at[pl.ds(first, W)],
            dst_ref=from_x.at[(1 - dx) // 2, pl.ds(0, W)],
            send_sem=send_main.at[(dx + 1) // 2],
            recv_sem=recv_main.at[(1 - dx) // 2],
            device_id=(gx + dx, gy),
            device_id_type=MESH,
        )

    def rim_copy(k, dx, dy):
        return pltpu.make_async_remote_copy(
            src_ref=send.at[span_x],
            dst_ref=landing(-dx, -dy),
            send_sem=send_rim.at[k],
            recv_sem=recv_rim.at[len(others) - 1 - k],
            device_id=(gx + dx, gy + dy),
            device_id_type=MESH,
        )

    def main_arrival(dx):
        return pltpu.make_async_remote_copy(
            src_ref=send.at[pl.ds(0, W)],
            dst_ref=from_x.at[(dx + 1) // 2, pl.ds(0, W)],
            send_sem=send_main.at[(dx + 1) // 2],
            recv_sem=recv_main.at[(dx + 1) // 2],
            device_id=(gx + dx, gy),
            device_id_type=MESH,
        )

    def rim_arrival(k, dx, dy):
        return pltpu.make_async_remote_copy(
            src_ref=send.at[span_x],
            dst_ref=landing(dx, dy),
            send_sem=send_rim.at[k],
            recv_sem=recv_rim.at[k],
            device_id=(gx + dx, gy + dy),
            device_id_type=MESH,
        )

    def masked(local_x, pairs, value):
        parts = []
        for pair in pairs:
            keep = jnp.broadcast_to(local_x // 2 == pair, (16, chunk))
            keep = jnp.where(keep, 1.0, 0.0).astype(BF)
            parts.append(value * jnp.concatenate([keep] * (2 * ROWS // 16), 0))
        return jnp.concatenate(parts, 0)

    def accumulate(total, left, right):
        total[...] += lax.dot_general(
            left, right, (((1,), (1,)), ((), ())), preferred_element_type=F32
        )

    def tile(pair, parity):
        at = (pair % (span_x // 4)) * 2 * ROWS
        cols = slice(parity * block_y, (parity + 1) * block_y)
        return acc[at : at + ROWS, cols] + acc[at + ROWS : at + 2 * ROWS, cols]

    def ready(first, last):
        for t in range(first, last):
            value = tile(t // 2, t % 2)
            if R <= t < R + block_x:
                value = value + jnp.where(inside, prior[t - R], 0.0)
            send[t] = value

    half = span_x // 4
    barrier = pltpu.get_barrier_semaphore()

    @pl.when(index == 0)
    def _():
        for dx, dy in others:
            @pl.when(present(dx, dy))
            def _():
                pl.semaphore_signal(
                    barrier, inc=1, device_id=(gx + dx, gy + dy), device_id_type=MESH
                )
        acc[...] = jnp.zeros_like(acc)
        acc_rim[...] = jnp.zeros_like(acc_rim)
        weighted[...] = jnp.zeros_like(weighted)
        prior[...] = jnp.zeros_like(prior)
        for x in range(block_x):
            prior[x, 0:species, :] = prior_weight * les[:, x, :]
            prior[x, species : species + 1, :] = jnp.full((1, block_y), prior_weight, F32)
            prior[x, species + 1 : species + 2, :] = 1.0 - jnp.exp(-rate[x : x + 1, :])
        for dx in (-1, 1):
            @pl.when(jnp.logical_not(has[dx][0]))
            def _():
                from_x[(dx + 1) // 2] = jnp.zeros((W + 1, ROWS, LANES), F32)
        for dx, dy in others:
            if dy != 0:
                @pl.when(jnp.logical_not(present(dx, dy)))
                def _():
                    landing(dx, dy)[...] = jnp.zeros((ROWS, LANES), F32)

    @pl.when(index < steps)
    def _():
        weighted[0:species, :] = comp[...] * mass[...]
        weighted[species : species + 1, :] = mass[...]
        value = weighted[...]
        high = value.astype(BF).astype(F32)
        both = jnp.concatenate([high, value - high], 0).astype(BF)
        split[index] = both
        local_x, inner, rim = positions(cell[...], block_x, block_y)
        column = jnp.where(inner < 0, -1, inner + (local_x % 2) * block_y)
        hot[index] = one_hot(column, 2 * block_y)
        hot_rim[...] = one_hot(rim, HALF)
        accumulate(acc, masked(local_x, range(half), both), hot[index])
        acc_rim[:, 0:HALF] += lax.dot_general(
            both, hot_rim[...], (((1,), (1,)), ((), ())), preferred_element_type=F32
        )

    @pl.when(index == steps - 1)
    def _():
        ready(0, W)
        rim_sum = acc_rim[0:ROWS, :] + acc_rim[ROWS:, :]
        for x in range(block_x):
            t = x + R
            low_at, high_at = t * W + R, side_size + t * W
            low, high = roll(prior[x], low_at), roll(prior[x], high_at + R)
            rim_sum += jnp.where((lane >= low_at) & (lane < low_at + R), low, 0.0)
            rim_sum += jnp.where((lane >= high_at) & (lane < high_at + R), high, 0.0)
        send[span_x] = rim_sum
        acc[...] = jnp.zeros_like(acc)
        number = (1 + (gx > 0).astype(jnp.int32) + (gx < counts[0] - 1).astype(jnp.int32)) * (
            1 + (gy > 0).astype(jnp.int32) + (gy < counts[1] - 1).astype(jnp.int32)
        ) - 1
        pl.semaphore_wait(barrier, number)

        @pl.when(has[-1][0])
        def _():
            main_copy(-1).start()

        for k, (dx, dy) in enumerate(others):
            @pl.when(present(dx, dy))
            def _():
                rim_copy(k, dx, dy).start()

    @pl.when(index >= steps)
    def _():
        at = index - steps
        local_x, _, _ = positions(cell[...], block_x, block_y)
        accumulate(acc, masked(local_x, range(half, 2 * half), split[at]), hot[at])

    @pl.when(index == 2 * steps - 1)
    def _():
        ready(W, span_x)

        @pl.when(has[1][0])
        def _():
            main_copy(1).start()

        for k, (dx, dy) in enumerate(others):
            @pl.when(present(dx, dy))
            def _():
                rim_arrival(k, dx, dy).wait_recv()

        @pl.when(has[1][0])
        def _():
            main_arrival(1).wait_recv()

        def finish(total):
            total_mass = total[species : species + 1, :]
            weight = jnp.where(total_mass > 0.0, total_mass, 1.0)
            weight = jnp.broadcast_to(weight, total.shape)
            return total / jnp.where(row < species, weight, 1.0)

        low_side = lane < side_size
        place_x = jnp.where(low_side, lane, lane - side_size)
        used = lane < 2 * side_size
        behind = used & (place_x < 2 * R * W)
        ahead = used & (place_x >= block_x * W)
        total = send[span_x]
        for dx, dy in others:
            mask = used if dx == 0 else behind if dx < 0 else ahead
            if dy != 0:
                mask = mask & (low_side if dy < 0 else jnp.logical_not(low_side))
            shift = dx * block_x * W + dy * side_size
            total = total + jnp.where(mask, roll(landing(dx, dy)[...], shift), 0.0)
        rim_value = finish(total)
        table[span_x] = rim_value

        def close(t):
            total = send[t]
            if t < W:
                total = total + from_x[0, t]
            if t >= block_x:
                total = total + from_x[1, t - block_x]
            value = finish(total)
            if R <= t < R + block_x:
                low_at, high_at = t * W + R, side_size + t * W
                value = jnp.where(lane < R, roll(rim_value, -low_at), value)
                value = jnp.where(
                    lane >= block_y - R, roll(rim_value, block_y - R - high_at), value
                )
            table[t] = value

        for t in range(W, span_x):
            close(t)

        @pl.when(has[-1][0])
        def _():
            main_arrival(-1).wait_recv()

        for t in range(W):
            close(t)
        for k, (dx, dy) in enumerate(others):
            @pl.when(present(dx, dy))
            def _():
                rim_copy(k, dx, dy).wait_send()
        for dx in (-1, 1):
            @pl.when(has[dx][0])
            def _():
                main_copy(dx).wait_send()


def stack_levels(target, plain, matrices):
    species = matrices.shape[1]
    plain[...] = jnp.zeros_like(plain)
    plain[0:species, 0:species] = matrices[2]
    plain[HALF : HALF + NS_MID, 0:NS_MID] = matrices[1, 0:NS_MID, 0:NS_MID]
    base = HALF + NS_MID
    plain[base : base + NS_LOW, 0:NS_LOW] = matrices[0, 0:NS_LOW, 0:NS_LOW]
    high, low = halves(plain[...])
    target[:, 0:HALF] = high
    target[:, HALF : 2 * HALF] = high
    target[:, 2 * HALF :] = low


def react_kernel(
    block_x, block_y, comp, cell, level, table, rate, implicit, out, means,
    left, left_rim, mixed, plain, left_rate, left_implicit,
):
    species = comp.shape[0]
    span_x = block_x + 2 * R
    piece = 2048

    @pl.when(pl.program_id(0) == 0)
    def _():
        mixed[...] = jnp.zeros_like(mixed)
        stack_levels(left_rate, plain, rate)
        stack_levels(left_implicit, plain, implicit)
        high, low = halves(table[0:span_x].reshape(span_x * ROWS, block_y))
        left[:, 0:block_y] = high
        left[:, block_y:] = low
        value = table[span_x]
        high = value.astype(BF).astype(F32)
        lane = lax.broadcasted_iota(jnp.int32, value.shape, 1)
        low = roll(value - high, HALF)
        left_rim[...] = jnp.where(lane < HALF, high, low).astype(BF)
        for x in range(block_x):
            means[:, x, :] = table[x + R, 0:species, :]

    def choose(test, yes, no):
        shape = (yes.shape[0] // 8, 8, piece)
        return jnp.where(test[None], yes.reshape(shape), no.reshape(shape)).reshape(yes.shape)

    def work(at):
        span = slice(at, at + piece)
        local_x, inner, rim = positions(cell[:, span], block_x, block_y)
        hot = one_hot(inner, block_y)
        hot_rim = one_hot(rim, HALF)
        rows = jnp.dot(left[...], jnp.concatenate([hot, hot], 0), preferred_element_type=F32)
        on_rim = jnp.dot(
            left_rim[...], jnp.concatenate([hot_rim, hot_rim], 0), preferred_element_type=F32
        )
        place = jnp.broadcast_to(local_x, (8, piece))
        parts = [rows[x * ROWS : (x + 1) * ROWS] for x in range(span_x)]
        bit = 1
        while len(parts) > 1:
            test = (place & bit) != 0
            paired = [
                choose(test, parts[i + 1], parts[i]) for i in range(0, len(parts) - 1, 2)
            ]
            parts = paired + parts[2 * len(paired) :]
            bit *= 2
        taken = choose(jnp.broadcast_to(inner, (8, piece)) < 0, on_rim, parts[0])
        factor = taken[species + 1 : species + 2]
        comp_value = comp[:, span]
        mixed[0:species, span] = comp_value - factor * (comp_value - taken[0:species])
        levels = jnp.broadcast_to(level[:, span], (8, piece))
        full, middle = levels == 2, levels == 1
        base = HALF + NS_MID

        def pick(value):
            return choose(
                full, value[0:NS_MID],
                choose(middle, value[HALF:base], value[base : base + NS_MID]),
            )

        high, low = halves(mixed[:, span])
        right = jnp.concatenate([high, low, high], 0)
        drive = jnp.dot(left_rate[...], right, preferred_element_type=F32)
        source = jnp.tanh(jnp.concatenate([pick(drive), drive[NS_MID:HALF]], 0))
        high, low = halves(source)
        right = jnp.concatenate([high, low, high], 0)
        change = jnp.dot(left_implicit[...], right, preferred_element_type=F32)
        rest = change[NS_MID:ROWS]
        rest = choose(full, rest, jnp.zeros_like(rest))
        out[0:NS_MID, span] = mixed[0:NS_MID, span] + chem_step * pick(change)
        out[NS_MID:, span] = mixed[NS_MID:species, span] + chem_step * rest[0 : species - NS_MID]

    for at in range(0, comp.shape[1], piece):
        work(at)


def per_device(
    counts, composition, particle_mass, particle_cell, particle_level,
    les_mean, mix_rate, rate_matrix, implicit_map,
):
    species, particles = composition.shape
    block_x, block_y = les_mean.shape[1], les_mean.shape[2]
    span_x = block_x + 2 * R
    whole = pl.BlockSpec(memory_space=pltpu.VMEM)
    chunk = 2048
    steps = particles // chunk
    left_rows = span_x // 4 * 2 * ROWS

    def first_pass(rows):
        return pl.BlockSpec((rows, chunk), lambda i: (0, jnp.minimum(i, steps - 1)))

    dma = pltpu.SemaphoreType.DMA
    tiles = (span_x + 1, ROWS, LANES)
    table = pl.pallas_call(
        functools.partial(sums_kernel, counts, steps, chunk, block_x, block_y),
        grid=(2 * steps,),
        out_shape=jax.ShapeDtypeStruct(tiles, F32),
        in_specs=[
            first_pass(species),
            first_pass(1),
            pl.BlockSpec((2, chunk), lambda i: (0, i % steps)),
            pl.BlockSpec(les_mean.shape, lambda i: (0, 0, 0)),
            pl.BlockSpec(mix_rate.shape, lambda i: (0, 0)),
        ],
        out_specs=pl.BlockSpec(tiles, lambda i: (0, 0, 0)),
        scratch_shapes=[
            pltpu.VMEM((steps, 2 * block_y, chunk), BF),
            pltpu.VMEM((HALF, chunk), BF),
            pltpu.VMEM((ROWS, chunk), F32),
            pltpu.VMEM((steps, 2 * ROWS, chunk), BF),
            pltpu.VMEM((left_rows, 2 * block_y), F32),
            pltpu.VMEM((2 * ROWS, LANES), F32),
            pltpu.VMEM(tiles, F32),
            pltpu.VMEM((block_x, ROWS, block_y), F32),
            pltpu.VMEM((2, W + 1, ROWS, LANES), F32),
            pltpu.VMEM((2, ROWS, LANES), F32),
            pltpu.VMEM((2, 2, ROWS, LANES), F32),
            dma((2,)), dma((2,)), dma((8,)), dma((8,)),
        ],
        compiler_params=pltpu.CompilerParams(
            collective_id=0, has_side_effects=True, vmem_limit_bytes=60 << 20
        ),
    )(composition, particle_mass[None], particle_cell, les_mean, mix_rate)
    stacked = HALF + 2 * NS_MID
    chunk = 2048

    def by_chunk(rows):
        return pl.BlockSpec((rows, chunk), lambda i: (0, i))

    def fixed(array):
        return pl.BlockSpec(array.shape, lambda i: (0,) * array.ndim)

    return pl.pallas_call(
        functools.partial(react_kernel, block_x, block_y),
        grid=(particles // chunk,),
        out_shape=(
            jax.ShapeDtypeStruct(composition.shape, F32),
            jax.ShapeDtypeStruct(les_mean.shape, F32),
        ),
        in_specs=[
            by_chunk(species), by_chunk(2), by_chunk(1),
            fixed(table), fixed(rate_matrix), fixed(implicit_map),
        ],
        out_specs=(by_chunk(species), fixed(les_mean)),
        scratch_shapes=[
            pltpu.VMEM((span_x * ROWS, 2 * block_y), BF),
            pltpu.VMEM((ROWS, LANES), BF),
            pltpu.VMEM((HALF, chunk), F32),
            pltpu.VMEM((stacked, HALF), F32),
            pltpu.VMEM((stacked, 3 * HALF), BF),
            pltpu.VMEM((stacked, 3 * HALF), BF),
        ],
        compiler_params=pltpu.CompilerParams(vmem_limit_bytes=40 << 20),
    )(composition, particle_cell, particle_level[None], table, rate_matrix, implicit_map)


def solution(mesh):
    placed = (
        P(None, ("gx", "gy")),
        P(("gx", "gy")),
        P(None, ("gx", "gy")),
        P(("gx", "gy")),
        P(None, "gx", "gy"),
        P("gx", "gy"),
        P(),
        P(),
    )
    return jax.shard_map(
        functools.partial(per_device, (mesh.shape["gx"], mesh.shape["gy"])),
        mesh=mesh,
        in_specs=placed,
        out_specs=(P(None, ("gx", "gy")), P(None, "gx", "gy")),
        check_vma=False,
    )
```

```python
import functools

import jax
import jax.numpy as jnp
from jax import lax
from jax.experimental import pallas as pl
from jax.experimental.pallas import tpu as pltpu
from jax.sharding import PartitionSpec as P

NS_LOW = 21
NS_MID = 24
R = 2
W = 2 * R
HALF = 64
ROWS = 56
LANES = 128

prior_weight = 16.0
chem_step = 0.5
BF = jnp.bfloat16
F32 = jnp.float32
MESH = pl.DeviceIdType.MESH


def halves(value):
    high = value.astype(BF)
    return high, (value - high.astype(F32)).astype(BF)


def roll(value, shift):
    return pltpu.roll(value, shift % value.shape[1], 1)


def positions(cell, block_x, block_y):
    local_x = cell[0:1] - (lax.axis_index("gx") * block_x - R)
    local_y = cell[1:2] - (lax.axis_index("gy") * block_y - R)
    low_rim = local_y < W
    on_rim = low_rim | (local_y >= block_y)
    rim = jnp.where(low_rim, local_y, local_y - block_y + (block_x + 2 * R) * W) + local_x * W
    return local_x, jnp.where(on_rim, -1, local_y - R), jnp.where(on_rim, rim, -1)


def one_hot(place, rows):
    sub = lax.broadcasted_iota(jnp.int32, (rows, place.shape[1]), 0)
    same = sub.astype(F32).astype(BF) == jnp.broadcast_to(
        place.astype(F32), (rows, place.shape[1])
    ).astype(BF)
    return jnp.where(same, jnp.ones((), BF), jnp.zeros((), BF))


def sums_kernel(
    counts, steps, chunk, block_x, block_y, comp, mass, cell, les, rate, table,
    hot, hot_rim, weighted, split, acc, acc_rim,
    send, prior, from_x, from_y, from_xy, send_main, recv_main, send_rim, recv_rim,
):
    species = comp.shape[0]
    span_x = block_x + 2 * R
    side_size = span_x * W
    gx, gy = lax.axis_index("gx"), lax.axis_index("gy")
    index = pl.program_id(0)
    has = {
        -1: (gx > 0, gy > 0),
        1: (gx < counts[0] - 1, gy < counts[1] - 1),
        0: (True, True),
    }
    others = [(dx, dy) for dx in (-1, 0, 1) for dy in (-1, 0, 1) if (dx, dy) != (0, 0)]
    lane = lax.broadcasted_iota(jnp.int32, (ROWS, LANES), 1)
    row = lax.broadcasted_iota(jnp.int32, (ROWS, LANES), 0)
    inside = (lane >= R) & (lane < block_y - R)

    def present(dx, dy):
        return jnp.logical_and(has[dx][0], has[dy][1])

    def landing(dx, dy):
        if dy == 0:
            return from_x.at[(dx + 1) // 2, W]
        if dx == 0:
            return from_y.at[(dy + 1) // 2]
        return from_xy.at[(dx + 1) // 2, (dy + 1) // 2]

    def main_copy(dx):
        first = 0 if dx < 0 else block_x
        return pltpu.make_async_remote_copy(
            src_ref=send.at[pl.ds(first, W)],
            dst_ref=from_x.at[(1 - dx) // 2, pl.ds(0, W)],
            send_sem=send_main.at[(dx + 1) // 2],
            recv_sem=recv_main.at[(1 - dx) // 2],
            device_id=(gx + dx, gy),
            device_id_type=MESH,
        )

    def rim_copy(k, dx, dy):
        return pltpu.make_async_remote_copy(
            src_ref=send.at[span_x],
            dst_ref=landing(-dx, -dy),
            send_sem=send_rim.at[k],
            recv_sem=recv_rim.at[len(others) - 1 - k],
            device_id=(gx + dx, gy + dy),
            device_id_type=MESH,
        )

    def main_arrival(dx):
        return pltpu.make_async_remote_copy(
            src_ref=send.at[pl.ds(0, W)],
            dst_ref=from_x.at[(dx + 1) // 2, pl.ds(0, W)],
            send_sem=send_main.at[(dx + 1) // 2],
            recv_sem=recv_main.at[(dx + 1) // 2],
            device_id=(gx + dx, gy),
            device_id_type=MESH,
        )

    def rim_arrival(k, dx, dy):
        return pltpu.make_async_remote_copy(
            src_ref=send.at[span_x],
            dst_ref=landing(dx, dy),
            send_sem=send_rim.at[k],
            recv_sem=recv_rim.at[k],
            device_id=(gx + dx, gy + dy),
            device_id_type=MESH,
        )

    def masked(local_x, pairs, value):
        parts = []
        for pair in pairs:
            keep = jnp.broadcast_to(local_x // 2 == pair, (16, chunk))
            keep = jnp.where(keep, 1.0, 0.0).astype(BF)
            parts.append(value * jnp.concatenate([keep] * (2 * ROWS // 16), 0))
        return jnp.concatenate(parts, 0)

    def accumulate(total, left, right):
        total[...] += lax.dot_general(
            left, right, (((1,), (1,)), ((), ())), preferred_element_type=F32
        )

    def tile(pair, parity):
        at = (pair % (span_x // 4)) * 2 * ROWS
        cols = slice(parity * block_y, (parity + 1) * block_y)
        return acc[at : at + ROWS, cols] + acc[at + ROWS : at + 2 * ROWS, cols]

    def ready(first, last):
        for t in range(first, last):
            value = tile(t // 2, t % 2)
            if R <= t < R + block_x:
                value = value + jnp.where(inside, prior[t - R], 0.0)
            send[t] = value

    half = span_x // 4
    barrier = pltpu.get_barrier_semaphore()

    @pl.when(index == 0)
    def _():
        for dx, dy in others:
            @pl.when(present(dx, dy))
            def _():
                pl.semaphore_signal(
                    barrier, inc=1, device_id=(gx + dx, gy + dy), device_id_type=MESH
                )
        acc[...] = jnp.zeros_like(acc)
        acc_rim[...] = jnp.zeros_like(acc_rim)
        weighted[...] = jnp.zeros_like(weighted)
        prior[...] = jnp.zeros_like(prior)
        for x in range(block_x):
            prior[x, 0:species, :] = prior_weight * les[:, x, :]
            prior[x, species : species + 1, :] = jnp.full((1, block_y), prior_weight, F32)
            prior[x, species + 1 : species + 2, :] = 1.0 - jnp.exp(-rate[x : x + 1, :])
        for dx in (-1, 1):
            @pl.when(jnp.logical_not(has[dx][0]))
            def _():
                from_x[(dx + 1) // 2] = jnp.zeros((W + 1, ROWS, LANES), F32)
        for dx, dy in others:
            if dy != 0:
                @pl.when(jnp.logical_not(present(dx, dy)))
                def _():
                    landing(dx, dy)[...] = jnp.zeros((ROWS, LANES), F32)

    @pl.when(index < steps)
    def _():
        weighted[0:species, :] = comp[...] * mass[...]
        weighted[species : species + 1, :] = mass[...]
        value = weighted[...]
        high = value.astype(BF).astype(F32)
        both = jnp.concatenate([high, value - high], 0).astype(BF)
        split[index] = both
        local_x, inner, rim = positions(cell[...], block_x, block_y)
        column = jnp.where(inner < 0, -1, inner + (local_x % 2) * block_y)
        hot[index] = one_hot(column, 2 * block_y)
        hot_rim[...] = one_hot(rim, HALF)
        accumulate(acc, masked(local_x, range(half), both), hot[index])
        acc_rim[:, 0:HALF] += lax.dot_general(
            both, hot_rim[...], (((1,), (1,)), ((), ())), preferred_element_type=F32
        )

    @pl.when(index == steps - 1)
    def _():
        ready(0, W)
        rim_sum = acc_rim[0:ROWS, :] + acc_rim[ROWS:, :]
        for x in range(block_x):
            t = x + R
            low_at, high_at = t * W + R, side_size + t * W
            low, high = roll(prior[x], low_at), roll(prior[x], high_at + R)
            rim_sum += jnp.where((lane >= low_at) & (lane < low_at + R), low, 0.0)
            rim_sum += jnp.where((lane >= high_at) & (lane < high_at + R), high, 0.0)
        send[span_x] = rim_sum
        acc[...] = jnp.zeros_like(acc)
        number = (1 + (gx > 0).astype(jnp.int32) + (gx < counts[0] - 1).astype(jnp.int32)) * (
            1 + (gy > 0).astype(jnp.int32) + (gy < counts[1] - 1).astype(jnp.int32)
        ) - 1
        pl.semaphore_wait(barrier, number)

        @pl.when(has[-1][0])
        def _():
            main_copy(-1).start()

        for k, (dx, dy) in enumerate(others):
            @pl.when(present(dx, dy))
            def _():
                rim_copy(k, dx, dy).start()

    @pl.when(index >= steps)
    def _():
        at = index - steps
        local_x, _, _ = positions(cell[...], block_x, block_y)
        accumulate(acc, masked(local_x, range(half, 2 * half), split[at]), hot[at])

    @pl.when(index == 2 * steps - 1)
    def _():
        ready(W, span_x)

        @pl.when(has[1][0])
        def _():
            main_copy(1).start()

        for k, (dx, dy) in enumerate(others):
            @pl.when(present(dx, dy))
            def _():
                rim_arrival(k, dx, dy).wait_recv()

        @pl.when(has[1][0])
        def _():
            main_arrival(1).wait_recv()

        def finish(total):
            total_mass = total[species : species + 1, :]
            weight = jnp.where(total_mass > 0.0, total_mass, 1.0)
            weight = jnp.broadcast_to(weight, total.shape)
            return total / jnp.where(row < species, weight, 1.0)

        low_side = lane < side_size
        place_x = jnp.where(low_side, lane, lane - side_size)
        used = lane < 2 * side_size
        behind = used & (place_x < 2 * R * W)
        ahead = used & (place_x >= block_x * W)
        total = send[span_x]
        for dx, dy in others:
            mask = used if dx == 0 else behind if dx < 0 else ahead
            if dy != 0:
                mask = mask & (low_side if dy < 0 else jnp.logical_not(low_side))
            shift = dx * block_x * W + dy * side_size
            total = total + jnp.where(mask, roll(landing(dx, dy)[...], shift), 0.0)
        rim_value = finish(total)
        table[span_x] = rim_value

        def close(t):
            total = send[t]
            if t < W:
                total = total + from_x[0, t]
            if t >= block_x:
                total = total + from_x[1, t - block_x]
            value = finish(total)
            if R <= t < R + block_x:
                low_at, high_at = t * W + R, side_size + t * W
                value = jnp.where(lane < R, roll(rim_value, -low_at), value)
                value = jnp.where(
                    lane >= block_y - R, roll(rim_value, block_y - R - high_at), value
                )
            table[t] = value

        for t in range(W, span_x):
            close(t)

        @pl.when(has[-1][0])
        def _():
            main_arrival(-1).wait_recv()

        for t in range(W):
            close(t)
        for k, (dx, dy) in enumerate(others):
            @pl.when(present(dx, dy))
            def _():
                rim_copy(k, dx, dy).wait_send()
        for dx in (-1, 1):
            @pl.when(has[dx][0])
            def _():
                main_copy(dx).wait_send()


def stack_levels(target, plain, matrices):
    species = matrices.shape[1]
    plain[...] = jnp.zeros_like(plain)
    plain[0:species, 0:species] = matrices[2]
    plain[HALF : HALF + NS_MID, 0:NS_MID] = matrices[1, 0:NS_MID, 0:NS_MID]
    base = HALF + NS_MID
    plain[base : base + NS_LOW, 0:NS_LOW] = matrices[0, 0:NS_LOW, 0:NS_LOW]
    high, low = halves(plain[...])
    target[:, 0:HALF] = high
    target[:, HALF : 2 * HALF] = high
    target[:, 2 * HALF :] = low


def react_kernel(
    block_x, block_y, comp, cell, level, table, rate, implicit, out, means,
    left, left_rim, mixed, plain, left_rate, left_implicit,
):
    species = comp.shape[0]
    span_x = block_x + 2 * R
    piece = 2048

    @pl.when(pl.program_id(0) == 0)
    def _():
        mixed[...] = jnp.zeros_like(mixed)
        stack_levels(left_rate, plain, rate)
        stack_levels(left_implicit, plain, implicit)
        high, low = halves(table[0:span_x].reshape(span_x * ROWS, block_y))
        left[:, 0:block_y] = high
        left[:, block_y:] = low
        value = table[span_x]
        high = value.astype(BF).astype(F32)
        lane = lax.broadcasted_iota(jnp.int32, value.shape, 1)
        low = roll(value - high, HALF)
        left_rim[...] = jnp.where(lane < HALF, high, low).astype(BF)
        for x in range(block_x):
            means[:, x, :] = table[x + R, 0:species, :]

    def choose(test, yes, no):
        shape = (yes.shape[0] // 8, 8, piece)
        return jnp.where(test[None], yes.reshape(shape), no.reshape(shape)).reshape(yes.shape)

    def work(at):
        span = slice(at, at + piece)
        local_x, inner, rim = positions(cell[:, span], block_x, block_y)
        hot = one_hot(inner, block_y)
        hot_rim = one_hot(rim, HALF)
        rows = jnp.dot(left[...], jnp.concatenate([hot, hot], 0), preferred_element_type=F32)
        on_rim = jnp.dot(
            left_rim[...], jnp.concatenate([hot_rim, hot_rim], 0), preferred_element_type=F32
        )
        place = jnp.broadcast_to(local_x, (8, piece))
        parts = [rows[x * ROWS : (x + 1) * ROWS] for x in range(span_x)]
        bit = 1
        while len(parts) > 1:
            test = (place & bit) != 0
            paired = [
                choose(test, parts[i + 1], parts[i]) for i in range(0, len(parts) - 1, 2)
            ]
            parts = paired + parts[2 * len(paired) :]
            bit *= 2
        taken = choose(jnp.broadcast_to(inner, (8, piece)) < 0, on_rim, parts[0])
        factor = taken[species + 1 : species + 2]
        comp_value = comp[:, span]
        mixed[0:species, span] = comp_value - factor * (comp_value - taken[0:species])
        levels = jnp.broadcast_to(level[:, span], (8, piece))
        full, middle = levels == 2, levels == 1
        base = HALF + NS_MID

        def pick(value):
            return choose(
                full, value[0:NS_MID],
                choose(middle, value[HALF:base], value[base : base + NS_MID]),
            )

        high, low = halves(mixed[:, span])
        right = jnp.concatenate([high, low, high], 0)
        drive = jnp.dot(left_rate[...], right, preferred_element_type=F32)
        source = jnp.tanh(jnp.concatenate([pick(drive), drive[NS_MID:HALF]], 0))
        high, low = halves(source)
        right = jnp.concatenate([high, low, high], 0)
        change = jnp.dot(left_implicit[...], right, preferred_element_type=F32)
        rest = change[NS_MID:ROWS]
        rest = choose(full, rest, jnp.zeros_like(rest))
        out[0:NS_MID, span] = mixed[0:NS_MID, span] + chem_step * pick(change)
        out[NS_MID:, span] = mixed[NS_MID:species, span] + chem_step * rest[0 : species - NS_MID]

    for at in range(0, comp.shape[1], piece):
        work(at)


def per_device(
    counts, composition, particle_mass, particle_cell, particle_level,
    les_mean, mix_rate, rate_matrix, implicit_map,
):
    species, particles = composition.shape
    block_x, block_y = les_mean.shape[1], les_mean.shape[2]
    span_x = block_x + 2 * R
    whole = pl.BlockSpec(memory_space=pltpu.VMEM)
    chunk = 4096
    steps = particles // chunk
    left_rows = span_x // 4 * 2 * ROWS

    def first_pass(rows):
        return pl.BlockSpec((rows, chunk), lambda i: (0, jnp.minimum(i, steps - 1)))

    dma = pltpu.SemaphoreType.DMA
    tiles = (span_x + 1, ROWS, LANES)
    table = pl.pallas_call(
        functools.partial(sums_kernel, counts, steps, chunk, block_x, block_y),
        grid=(2 * steps,),
        out_shape=jax.ShapeDtypeStruct(tiles, F32),
        in_specs=[
            first_pass(species),
            first_pass(1),
            pl.BlockSpec((2, chunk), lambda i: (0, i % steps)),
            pl.BlockSpec(les_mean.shape, lambda i: (0, 0, 0)),
            pl.BlockSpec(mix_rate.shape, lambda i: (0, 0)),
        ],
        out_specs=pl.BlockSpec(tiles, lambda i: (0, 0, 0)),
        scratch_shapes=[
            pltpu.VMEM((steps, 2 * block_y, chunk), BF),
            pltpu.VMEM((HALF, chunk), BF),
            pltpu.VMEM((ROWS, chunk), F32),
            pltpu.VMEM((steps, 2 * ROWS, chunk), BF),
            pltpu.VMEM((left_rows, 2 * block_y), F32),
            pltpu.VMEM((2 * ROWS, LANES), F32),
            pltpu.VMEM(tiles, F32),
            pltpu.VMEM((block_x, ROWS, block_y), F32),
            pltpu.VMEM((2, W + 1, ROWS, LANES), F32),
            pltpu.VMEM((2, ROWS, LANES), F32),
            pltpu.VMEM((2, 2, ROWS, LANES), F32),
            dma((2,)), dma((2,)), dma((8,)), dma((8,)),
        ],
        compiler_params=pltpu.CompilerParams(
            collective_id=0, has_side_effects=True, vmem_limit_bytes=60 << 20
        ),
    )(composition, particle_mass[None], particle_cell, les_mean, mix_rate)
    stacked = HALF + 2 * NS_MID
    chunk = 2048

    def by_chunk(rows):
        return pl.BlockSpec((rows, chunk), lambda i: (0, i))

    def fixed(array):
        return pl.BlockSpec(array.shape, lambda i: (0,) * array.ndim)

    return pl.pallas_call(
        functools.partial(react_kernel, block_x, block_y),
        grid=(particles // chunk,),
        out_shape=(
            jax.ShapeDtypeStruct(composition.shape, F32),
            jax.ShapeDtypeStruct(les_mean.shape, F32),
        ),
        in_specs=[
            by_chunk(species), by_chunk(2), by_chunk(1),
            fixed(table), fixed(rate_matrix), fixed(implicit_map),
        ],
        out_specs=(by_chunk(species), fixed(les_mean)),
        scratch_shapes=[
            pltpu.VMEM((span_x * ROWS, 2 * block_y), BF),
            pltpu.VMEM((ROWS, LANES), BF),
            pltpu.VMEM((HALF, chunk), F32),
            pltpu.VMEM((stacked, HALF), F32),
            pltpu.VMEM((stacked, 3 * HALF), BF),
            pltpu.VMEM((stacked, 3 * HALF), BF),
        ],
        compiler_params=pltpu.CompilerParams(vmem_limit_bytes=40 << 20),
    )(composition, particle_cell, particle_level[None], table, rate_matrix, implicit_map)


def solution(mesh):
    placed = (
        P(None, ("gx", "gy")),
        P(("gx", "gy")),
        P(None, ("gx", "gy")),
        P(("gx", "gy")),
        P(None, "gx", "gy"),
        P("gx", "gy"),
        P(),
        P(),
    )
    return jax.shard_map(
        functools.partial(per_device, (mesh.shape["gx"], mesh.shape["gy"])),
        mesh=mesh,
        in_specs=placed,
        out_specs=(P(None, ("gx", "gy")), P(None, "gx", "gy")),
        check_vma=False,
    )
```
